32 devices in a mesh: batch: 4 (over y, x), proto: 8 (over z, core).
Axes of the slice: x: 2, y: 2, z: 4, core: 2. Of those that a mesh axis runs over, the one named last changes fastest.
Arguments:
- teacher_emb: bfloat16 [256, 2048], P('proto', 'batch'), may hold values from -22 to 22
- student_emb: bfloat16 [256, 2048], P('proto', 'batch'), may hold values from -6 to 6
- prototypes: bfloat16 [256, 65536], P('batch', 'proto'), may hold values from -16 to 16
Outputs:
- grad_proto: float32 [256, 65536], P('batch', 'proto')
- grad_student: float32 [256, 2048], P('proto', 'batch')
- loss: float32 [], replicated
The draws below stay inside these ranges and needn't reach their ends.
All inputs are finite; a program needn't handle non-finite values.
Results may differ from the reference program's by a relative error of at most 0.00055.
The reference program's roundings to bfloat16 on the way (of `proto_unit` and `grad_logit`) count: a program that leaves them out, or rounds other values in their place, can miss the bound.
Values may be sent and summed in bfloat16 or wider, within the bound.
No kernel may reach another device: no remote copies, remote signals or barrier semaphores. Data moves between devices by JAX's collectives and lax.ppermute only.
A program may use at most 128 MiB of HBM per device.

```python
import jax
import jax.numpy as jnp
from jax import lax

K = 256
PROTOS = 65536
ROWS_DEV = 512
ITERS = 3
CROPS = 2048


def common_axis(key):
    return jnp.clip(jax.random.normal(jax.random.fold_in(key, 7), (K, 1), jnp.float32), -4.0, 4.0)


def draw_teacher_emb(key, part):
    direction = common_axis(key)
    noise = jnp.clip(jax.random.normal(jax.random.fold_in(key, 1), (K, CROPS), jnp.float32), -6.0, 6.0)
    reach = 3.0
    trend = reach * jnp.arange(CROPS, dtype=jnp.float32) / CROPS
    return (noise + trend[None, :] * direction).astype(jnp.bfloat16)


def draw_prototypes(key, part):
    direction = common_axis(key)
    noise = jnp.clip(jax.random.normal(jax.random.fold_in(key, 2), (K, PROTOS), jnp.float32), -6.0, 6.0)
    jitter = jax.random.uniform(jax.random.fold_in(key, 3), (PROTOS,), jnp.float32, -1.0, 1.0)
    lean = 1.5 * (2.0 * jnp.arange(PROTOS, dtype=jnp.float32) / PROTOS - 1.0) + jitter
    return (noise + lean[None, :] * direction).astype(jnp.bfloat16)


def spiked(result, key, source, target, parts, factor):
    def block_of(dim):
        return (jnp.arange(result.shape[dim]) // (result.shape[dim] // parts)).reshape((-1,) + (1,) * (result.ndim - 1 - dim))

    first = jax.random.permutation(key, parts)[block_of(target)]
    far = (block_of(target) + parts // 2) % parts
    return jnp.where((block_of(source) == first) | (block_of(source) == far), factor * result, result)


def block_levels(stream_key, shape, cuts, low, top_value):
    gain = 1.0
    for axis_at, blocks in cuts:
        draws = jax.random.uniform(jax.random.fold_in(jax.random.fold_in(stream_key, 6), axis_at), (blocks,), jnp.float32, low / len(cuts), top_value / len(cuts))
        gain = gain * jnp.repeat(jnp.exp(draws), shape[axis_at] // blocks).reshape((-1,) + (1,) * (len(shape) - 1 - axis_at))
    return gain


def noise_with(stream_key, extent, deviation, limit, cuts, heavy, kind=jnp.bfloat16):
    entries = deviation * jax.random.normal(stream_key, extent, jnp.float32)
    if cuts:
        entries = entries * block_levels(stream_key, extent, cuts, -0.22, 0.18)
    return jnp.clip(spiked(entries, jax.random.fold_in(stream_key, 3), *heavy), -limit, limit).astype(kind)


def setup_inputs(seed: int = 0) -> dict:
    key_of = jax.random.split(jax.random.key(seed), 4)
    teacher_emb = draw_teacher_emb(jax.random.fold_in(key_of[3], 71), 0)
    student_emb = noise_with(key_of[1], (K, CROPS), 1.0, 6.0, ((0, 8), (1, 4)), (1, 0, 8, 2.0))
    prototypes = draw_prototypes(jax.random.fold_in(key_of[3], 71), 0)
    return dict(teacher_emb=teacher_emb, student_emb=student_emb, prototypes=prototypes)


teacher_temp = 0.07
student_temp = 0.1
epsilon = 1e-06

def unit(matrix):
    values = matrix.astype(jnp.float32)
    factor = lax.rsqrt(lax.optimization_barrier(jnp.sum(values * values, axis=0, keepdims=True)) + epsilon)
    return ((values * factor).astype(jnp.bfloat16), factor)

def cosine(left, right):
    return lax.dot_general(left, right, (((0,), (0,)), ((), ())), preferred_element_type=jnp.float32)

def reference(teacher_emb, student_emb, prototypes):
    proto_unit, proto_scale = unit(prototypes)
    teacher_unit, unused = unit(teacher_emb)
    student_unit, student_scale = unit(student_emb)
    width = teacher_emb.shape[0]
    total_rows = teacher_emb.shape[1]
    count = total_rows // ROWS_DEV

    def blocks(matrix):
        return matrix.reshape(width, count, ROWS_DEV).transpose(1, 0, 2)
    teacher_blocks = blocks(teacher_unit)
    student_blocks = blocks(student_unit)

    def expo_of(block):
        return jnp.exp(cosine(block, proto_unit) / teacher_temp)
    crop_scale = jnp.ones((count, ROWS_DEV), jnp.float32)
    proto_inv = jnp.ones((PROTOS,), jnp.float32)
    for iteration in range(ITERS):

        def add_column(carry, item):
            block, weights = item
            return (carry + jnp.dot(weights, expo_of(block), precision=lax.Precision.HIGHEST), None)
        column_sum, unused_out = lax.scan(add_column, jnp.zeros((PROTOS,), jnp.float32), (teacher_blocks, crop_scale))
        proto_inv = 1.0 / column_sum

        def row_of(block):
            return jnp.dot(expo_of(block), proto_inv, precision=lax.Precision.HIGHEST)
        crop_scale = 1.0 / lax.map(row_of, teacher_blocks)

    def final(carry, item):
        grad_sum, loss_sum = carry
        teacher_block, student_block, weights = item
        targets = expo_of(teacher_block) * proto_inv[None, :] * weights[:, None]
        logits = cosine(student_block, proto_unit) / student_temp
        logp = logits - jnp.log(lax.optimization_barrier(jnp.sum(jnp.exp(logits), axis=1, keepdims=True)))
        loss_sum = loss_sum - jnp.sum(targets * logp)
        grad_logit = ((jnp.exp(logp) - targets) / (total_rows * student_temp)).astype(jnp.bfloat16)
        grad_sum = grad_sum + jnp.dot(student_block, grad_logit, preferred_element_type=jnp.float32)
        crop_part = lax.dot_general(proto_unit, grad_logit, (((1,), (1,)), ((), ())), preferred_element_type=jnp.float32)
        return ((grad_sum, loss_sum), crop_part)
    start = (jnp.zeros((width, PROTOS), jnp.float32), jnp.zeros((), jnp.float32))
    (grad_unit_proto, loss_sum), crop_parts = lax.scan(final, start, (teacher_blocks, student_blocks, crop_scale))
    grad_unit_crop = crop_parts.transpose(1, 0, 2).reshape(width, total_rows)
    proto_values = proto_unit.astype(jnp.float32)
    proto_dot = lax.optimization_barrier(jnp.sum(proto_values * grad_unit_proto, axis=0, keepdims=True))
    grad_proto = (grad_unit_proto - proto_values * proto_dot) * proto_scale
    student_values = student_unit.astype(jnp.float32)
    crop_dot = lax.optimization_barrier(jnp.sum(student_values * grad_unit_crop, axis=0, keepdims=True))
    grad_student = (grad_unit_crop - student_values * crop_dot) * student_scale
    return (grad_proto, grad_student, loss_sum / total_rows)
```

```python
import functools
import math

import jax
import jax.numpy as jnp
from jax import lax
from jax.experimental import pallas as pl
from jax.experimental.pallas import tpu as pltpu
from jax.sharding import PartitionSpec as P

ITERS = 3
CORES = 2
AXES = ("batch", "proto")

teacher_temp = 0.07
student_temp = 0.1
epsilon = 1e-06
LOG2E = 1.0 / math.log(2.0)
T_GAIN = LOG2E / teacher_temp
S_GAIN = LOG2E / student_temp

SMEM = pl.BlockSpec(memory_space=pltpu.SMEM)
VMEM = pl.BlockSpec(memory_space=pltpu.VMEM)


def whole(shape):
    return pl.BlockSpec(shape, lambda *grid: (0,) * len(shape))


def params(megabytes=48):
    return pltpu.CompilerParams(vmem_limit_bytes=megabytes << 20)


def swap(x, over_batch, over_z, over_core):
    batch, proto = lax.axis_size("batch"), lax.axis_size("proto")
    pairs = []
    for b in range(batch):
        for p in range(proto):
            other = p ^ (over_z * CORES + over_core)
            pairs.append((b * proto + p, (b ^ over_batch) * proto + other))
    return lax.ppermute(x, AXES, pairs)


def z_masks(nz):
    return [(2 << i) - 1 for i in range(nz.bit_length() - 1)]


def gather_crops(x):
    batch = lax.axis_size("batch")
    nz = lax.axis_size("proto") // CORES
    pieces = jnp.stack([x] + [swap(x, o, 0, 0) for o in range(1, batch)])
    found = []
    masks = z_masks(nz)
    for first, order in ((0, masks), (batch // 2, masks[::-1])):
        held = pieces[None, first : first + batch // 2]
        offsets = [0]
        for mask in order:
            held = jnp.concatenate([held, swap(held, 0, mask, 0)], axis=0)
            offsets = offsets + [o ^ mask for o in offsets]
        found.append((held, offsets, first, 0))
        found.append((swap(held, 0, 0, 1), offsets, first, 1))
    return found


def unit_crops_body(plan, at_ref, *refs):
    pieces, (unit_ref, scale_ref, raw) = refs[: len(plan)], refs[len(plan) :]
    j, z, c = at_ref[0], at_ref[1], at_ref[2]
    for ref, (offsets, first, core) in zip(pieces, plan):
        rows, cols = ref.shape[2:]
        for i, oz in enumerate(offsets):
            top = pl.multiple_of(((z ^ oz) * CORES + (c ^ core)) * rows, rows)
            for k in range(ref.shape[1]):
                left = pl.multiple_of((j ^ (first + k)) * cols, cols)
                raw[pl.ds(top, rows), pl.ds(left, cols)] = ref[i, k]
    step = ref.shape[3]
    for left in range(0, raw.shape[1], step):
        values = raw[:, left : left + step].astype(jnp.float32)
        factor = lax.rsqrt(jnp.sum(values * values, axis=0, keepdims=True) + epsilon)
        unit_ref[:, left : left + step] = (values * factor).astype(jnp.bfloat16)
        scale_ref[:, left : left + step] = factor


def unit_crops(at, found, width, crops):
    plan = [(offsets, first, core) for _, offsets, first, core in found]
    return pl.pallas_call(
        functools.partial(unit_crops_body, plan),
        out_shape=(
            jax.ShapeDtypeStruct((width, crops), jnp.bfloat16),
            jax.ShapeDtypeStruct((1, crops), jnp.float32),
        ),
        in_specs=[SMEM] + [VMEM] * len(found),
        out_specs=(VMEM, VMEM),
        scratch_shapes=[pltpu.VMEM((width, crops), jnp.bfloat16)],
        compiler_params=params(),
        name="unit_crops",
    )(at, *[piece for piece, *_ in found])


def unit_protos_body(at_ref, *refs):
    blocks, (unit_ref, turned_ref, scale_ref, raw) = refs[:-4], refs[-4:]
    j = at_ref[0]
    rows = blocks[0].shape[0]
    for o, ref in enumerate(blocks):
        top = pl.multiple_of((j ^ o) * rows, rows)
        raw[pl.ds(top, rows), :] = ref[...]
    values = raw[...].astype(jnp.float32)
    factor = lax.rsqrt(jnp.sum(values * values, axis=0, keepdims=True) + epsilon)
    unit = (values * factor).astype(jnp.bfloat16)
    unit_ref[...] = unit
    turned_ref[...] = unit.T
    scale_ref[...] = factor


def unit_protos(at, blocks):
    rows, protos = blocks[0].shape
    width = rows * len(blocks)
    step = min(512, protos)
    return pl.pallas_call(
        unit_protos_body,
        grid=(protos // step,),
        out_shape=(
            jax.ShapeDtypeStruct((width, protos), jnp.bfloat16),
            jax.ShapeDtypeStruct((protos, width), jnp.bfloat16),
            jax.ShapeDtypeStruct((1, protos), jnp.float32),
        ),
        in_specs=[SMEM] + [pl.BlockSpec((rows, step), lambda i: (0, i))] * len(blocks),
        out_specs=(
            pl.BlockSpec((width, step), lambda i: (0, i)),
            pl.BlockSpec((step, width), lambda i: (i, 0)),
            pl.BlockSpec((1, step), lambda i: (0, i)),
        ),
        scratch_shapes=[pltpu.VMEM((width, step), jnp.bfloat16)],
        compiler_params=params(),
        name="unit_protos",
    )(at, *blocks)


def scores(turned_ref, unit_ref):
    return jnp.dot(turned_ref[...], unit_ref[...], preferred_element_type=jnp.float32)


def add_rows(row_ref, values):
    total = jnp.sum(values, axis=0, keepdims=True)

    @pl.when(pl.program_id(0) == 0)
    def _():
        row_ref[...] = total

    @pl.when(pl.program_id(0) > 0)
    def _():
        row_ref[...] += total


def sinkhorn_body(turned_ref, teacher_ref, crop_ref, row_ref, inv_ref):
    mass = jnp.exp2(scores(turned_ref, teacher_ref) * T_GAIN) * crop_ref[...]
    inv = 1.0 / jnp.sum(mass, axis=1, keepdims=True)
    inv_ref[...] = inv
    add_rows(row_ref, mass * inv)


def first_body(turned_ref, teacher_ref, row_ref):
    mass = jnp.exp2(scores(turned_ref, teacher_ref) * T_GAIN)
    add_rows(row_ref, mass * (1.0 / jnp.sum(mass, axis=1, keepdims=True)))


def softmax_body(turned_ref, student_ref, row_ref):
    add_rows(row_ref, jnp.exp2(scores(turned_ref, student_ref) * S_GAIN))


def sweep(body, name, turned, *rest, inverse=False):
    protos, width = turned.shape
    step = min(256, protos)
    crops = rest[0].shape[1]
    row = jax.ShapeDtypeStruct((1, crops), jnp.float32)
    inv = jax.ShapeDtypeStruct((protos, 1), jnp.float32)
    return pl.pallas_call(
        body,
        grid=(protos // step,),
        out_shape=(row, inv) if inverse else row,
        in_specs=[pl.BlockSpec((step, width), lambda i: (i, 0))] + [whole(x.shape) for x in rest],
        out_specs=(whole((1, crops)), pl.BlockSpec((step, 1), lambda i: (i, 0)))
        if inverse
        else whole((1, crops)),
        compiler_params=params(),
        name=name,
    )(turned, *rest)


def grads_body(
    plan,
    grain,
    at_ref,
    turned_ref,
    protos_ref,
    inv_ref,
    proto_scale_ref,
    teacher_ref,
    student_ref,
    crop_ref,
    total_ref,
    crop_scale_ref,
    proto_out,
    crop_out,
    loss_ref,
    crop_sum,
    loss_sum,
):
    nb, nz, rows, cols = plan
    j, z, c = at_ref[0], at_ref[1], at_ref[2]
    first = pl.program_id(0) == 0
    log_total = jnp.log(total_ref[...])
    targets = jnp.exp2(scores(turned_ref, teacher_ref) * T_GAIN) * crop_ref[...] * inv_ref[...]
    logp = scores(turned_ref, student_ref) * (1.0 / student_temp) - log_total
    grad = ((jnp.exp(logp) - targets) * (1.0 / grain)).astype(jnp.bfloat16)
    add_rows(loss_sum, targets * logp)
    protos = protos_ref[...]
    by_proto = lax.dot_general(
        student_ref[...], grad, (((1,), (1,)), ((), ())), preferred_element_type=jnp.float32
    )
    values = protos.astype(jnp.float32)
    radial = jnp.sum(values * by_proto, axis=0, keepdims=True)
    result = (by_proto - values * radial) * proto_scale_ref[...]
    wide = result.shape[0] // nb
    for o in range(nb):
        for source in range(nb):
            @pl.when((j ^ o) == source)
            def _(o=o, source=source):
                proto_out[o] = result[source * wide : (source + 1) * wide, :]
    part = jnp.dot(protos, grad, preferred_element_type=jnp.float32)

    @pl.when(first)
    def _():
        crop_sum[...] = part

    @pl.when(jnp.logical_not(first))
    def _():
        crop_sum[...] += part

    @pl.when(pl.program_id(0) == pl.num_programs(0) - 1)
    def _():
        loss_ref[...] = jnp.sum(loss_sum[...], axis=1, keepdims=True)
        student = student_ref[...].astype(jnp.float32)
        total = crop_sum[...]
        dot = jnp.sum(student * total, axis=0, keepdims=True)
        crop_sum[...] = (total - student * dot) * crop_scale_ref[...]
        for oc in range(CORES):
            for oz in range(nz):
                top = pl.multiple_of(((z ^ oz) * CORES + (c ^ oc)) * rows, rows)
                for ob in range(nb):
                    left = pl.multiple_of((j ^ ob) * cols, cols)
                    crop_out[oc, oz, ob] = crop_sum[pl.ds(top, rows), pl.ds(left, cols)]


def gradients(at, grain, sizes, turned, protos, inv, proto_scale, teacher, student, crop, total, crop_scale):
    nb, nz = sizes
    width, count = protos.shape
    crops = teacher.shape[1]
    step = min(256, count)
    rows, cols = width // (nz * CORES), crops // nb
    wide = width // nb
    return pl.pallas_call(
        functools.partial(grads_body, (nb, nz, rows, cols), grain),
        grid=(count // step,),
        out_shape=(
            jax.ShapeDtypeStruct((nb, wide, count), jnp.float32),
            jax.ShapeDtypeStruct((CORES, nz, nb, rows, cols), jnp.float32),
            jax.ShapeDtypeStruct((1, 1), jnp.float32),
        ),
        in_specs=[
            SMEM,
            pl.BlockSpec((step, width), lambda i: (i, 0)),
            pl.BlockSpec((width, step), lambda i: (0, i)),
            pl.BlockSpec((step, 1), lambda i: (i, 0)),
            pl.BlockSpec((1, step), lambda i: (0, i)),
        ]
        + [whole(x.shape) for x in (teacher, student, crop, total, crop_scale)],
        out_specs=(
            pl.BlockSpec((nb, wide, step), lambda i: (0, 0, i)),
            whole((CORES, nz, nb, rows, cols)),
            whole((1, 1)),
        ),
        scratch_shapes=[
            pltpu.VMEM((width, crops), jnp.float32),
            pltpu.VMEM((1, crops), jnp.float32),
        ],
        compiler_params=params(56),
        name="gradients",
    )(at, turned, protos, inv, proto_scale, teacher, student, crop, total, crop_scale)


def sum_everywhere(rows):
    n, crops = rows.shape
    devices = lax.axis_size("batch") * lax.axis_size("proto")
    core = lax.axis_index("proto") % CORES
    rows = rows + swap(rows, 0, 0, 1)
    half = lax.dynamic_index_in_dim(rows.reshape(n, CORES, crops // CORES), core, 1, keepdims=False)
    sent = jnp.broadcast_to(half[None], (devices, n, crops // CORES))
    got = lax.all_to_all(sent, AXES, 0, 0)
    got = got.reshape(devices // CORES, CORES, n, crops // CORES).sum(axis=0)
    return got.transpose(1, 0, 2).reshape(n, crops)


def scatter_crops(parts, nz, nb):
    kept = parts[0] + swap(parts[1], 0, 0, 1)
    masks = z_masks(nz)
    halves = []
    for first, order in ((0, masks), (nb // 2, masks[::-1])):
        held = {o: kept[o, first : first + nb // 2] for o in range(nz)}
        for i, mask in enumerate(order):
            span = [0]
            for later in order[i + 1 :]:
                span = span + [o ^ later for o in span]
            sent = jnp.stack([held[o ^ mask] for o in span])
            got = swap(sent, 0, mask, 0)
            held = {o: held[o] + got[n] for n, o in enumerate(span)}
        halves.append(held[0])
    mine = jnp.concatenate(halves, axis=0)
    return sum([swap(mine[o], o, 0, 0) for o in range(1, nb)], mine[0])


def shards(teacher_emb, student_emb, prototypes):
    nb, nproto = lax.axis_size("batch"), lax.axis_size("proto")
    nz = nproto // CORES
    j, p = lax.axis_index("batch"), lax.axis_index("proto")
    at = jnp.stack([j, p // CORES, p % CORES]).astype(jnp.int32)
    width = teacher_emb.shape[0] * nproto
    crops = teacher_emb.shape[1] * nb
    rows, local = prototypes.shape
    count = local // nb

    def columns(o):
        return lax.dynamic_slice_in_dim(prototypes, (j ^ o) * count, count, 1)

    blocks = [columns(0)] + [swap(columns(o), o, 0, 0) for o in range(1, nb)]
    protos, turned, proto_scale = unit_protos(at, blocks)
    teacher, unused = unit_crops(at, gather_crops(teacher_emb), width, crops)
    student, crop_unit_scale = unit_crops(at, gather_crops(student_emb), width, crops)

    crop_scale = 1.0 / sum_everywhere(sweep(first_body, "first", turned, teacher))
    softmax_part = sweep(softmax_body, "softmax", turned, student)
    for iteration in range(1, ITERS):
        total, inv = sweep(sinkhorn_body, "sinkhorn", turned, teacher, crop_scale, inverse=True)
        if iteration == 1:
            both = sum_everywhere(jnp.concatenate([total, softmax_part], axis=0))
            total, softmax_total = both[:1], both[1:]
        else:
            total = sum_everywhere(total)
        crop_scale = crop_scale / total
    grain = crops * student_temp
    proto_parts, crop_parts, loss_part = gradients(
        at, grain, (nb, nz), turned, protos, inv, proto_scale, teacher, student, crop_scale,
        softmax_total, crop_unit_scale,
    )
    grad_proto = jnp.zeros((rows, local), jnp.float32)
    for o in range(nb):
        got = swap(proto_parts[o], o, 0, 0) if o else proto_parts[0]
        grad_proto = lax.dynamic_update_slice_in_dim(grad_proto, got, (j ^ o) * count, 1)
    grad_student = scatter_crops(crop_parts, nz, nb)
    loss = jnp.broadcast_to(loss_part, (1, 128))
    loss = loss + swap(loss, 0, 0, 1)
    for mask in z_masks(nz):
        loss = loss + swap(loss, 0, mask, 0)
    for i in range(nb.bit_length() - 1):
        loss = loss + swap(loss, 1 << i, 0, 0)
    return (grad_proto, grad_student, -loss[0, 0] / crops)


def solution(mesh):
    in_specs = (P("proto", "batch"), P("proto", "batch"), P("batch", "proto"))
    out_specs = (P("batch", "proto"), P("proto", "batch"), P())
    return jax.shard_map(shards, mesh=mesh, in_specs=in_specs, out_specs=out_specs, check_vma=False)
```

```python
import functools
import math

import jax
import jax.numpy as jnp
from jax import lax
from jax.experimental import pallas as pl
from jax.experimental.pallas import tpu as pltpu
from jax.sharding import PartitionSpec as P


ITERS = 3
CORES = 2
AXES = ("batch", "proto")

teacher_temp = 0.07
student_temp = 0.1
epsilon = 1e-06
LOG2E = 1.0 / math.log(2.0)
T_GAIN = LOG2E / teacher_temp
S_GAIN = LOG2E / student_temp

SMEM = pl.BlockSpec(memory_space=pltpu.SMEM)
VMEM = pl.BlockSpec(memory_space=pltpu.VMEM)


def params(megabytes=24):
    return pltpu.CompilerParams(vmem_limit_bytes=megabytes << 20)


def swap(x, over_batch, over_z, over_core):
    batch, proto = lax.axis_size("batch"), lax.axis_size("proto")
    pairs = []
    for b in range(batch):
        for p in range(proto):
            other = p ^ (over_z * CORES + over_core)
            pairs.append((b * proto + p, (b ^ over_batch) * proto + other))
    return lax.ppermute(x, AXES, pairs)


def z_masks(nz):
    return [(2 << i) - 1 for i in range(nz.bit_length() - 1)]


def join(parts):
    return jnp.concatenate(parts, axis=0)


def gather_crops(x):
    batch = lax.axis_size("batch")
    nz = lax.axis_size("proto") // CORES
    pieces = join([x[None]] + [swap(x[None], o, 0, 0) for o in range(1, batch)])
    masks = z_masks(nz)
    found = []
    for first, order in ((0, masks), (batch // 2, masks[::-1])):
        held = pieces[None, first : first + batch // 2]
        offsets = [0]
        for mask in order:
            held = join([held, swap(held, 0, mask, 0)])
            offsets = offsets + [o ^ mask for o in offsets]
        found.append((held, offsets, first, 0))
        found.append((swap(held, 0, 0, 1), offsets, first, 1))
    return found


def unit_crops_body(plan, at_ref, *refs):
    pieces, (unit_ref, scale_ref, raw, sems) = refs[: len(plan)], refs[len(plan) :]
    j, z, c = at_ref[0], at_ref[1], at_ref[2]
    copies = []
    for ref, (offsets, first, core) in zip(pieces, plan):
        rows, cols = ref.shape[2:]
        for i, oz in enumerate(offsets):
            top = pl.multiple_of(((z ^ oz) * CORES + (c ^ core)) * rows, rows)
            for k in range(ref.shape[1]):
                left = pl.multiple_of((j ^ (first + k)) * cols, cols)
                target = raw.at[pl.ds(top, rows), pl.ds(left, cols)]
                copies.append(pltpu.make_async_copy(ref.at[i, k], target, sems.at[len(copies)]))
                copies[-1].start()
    for copy in copies:
        copy.wait()
    for left in range(0, raw.shape[1], cols):
        part = slice(left, left + cols)
        values = raw[:, part].astype(jnp.float32)
        factor = lax.rsqrt(jnp.sum(values * values, axis=0, keepdims=True) + epsilon)
        unit_ref[:, part] = (values * factor).astype(jnp.bfloat16)
        scale_ref[:, part] = factor


def unit_crops(at, found, width, crops, megabytes):
    plan = [(offsets, first, core) for _, offsets, first, core in found]
    copies = sum(piece.shape[0] * piece.shape[1] for piece, *_ in found)
    return pl.pallas_call(
        functools.partial(unit_crops_body, plan),
        out_shape=(
            jax.ShapeDtypeStruct((width, crops), jnp.bfloat16),
            jax.ShapeDtypeStruct((1, crops), jnp.float32),
        ),
        in_specs=[SMEM] + [pl.BlockSpec(memory_space=pltpu.HBM)] * len(found),
        out_specs=(VMEM, VMEM),
        scratch_shapes=[
            pltpu.VMEM((width, crops), jnp.bfloat16),
            pltpu.SemaphoreType.DMA((copies,)),
        ],
        compiler_params=params(megabytes),
    )(at, *[piece for piece, *_ in found])


def unit_protos_body(at_ref, *refs):
    blocks, (turned_ref, scale_ref, raw) = refs[:-3], refs[-3:]
    j = at_ref[0]
    rows, step = blocks[0].shape[0], raw.shape[1]
    for low in range(0, blocks[0].shape[1], step):
        part = slice(low, low + step)
        for o, ref in enumerate(blocks):
            top = pl.multiple_of((j ^ o) * rows, rows)
            raw[pl.ds(top, rows), :] = ref[:, part]
        values = raw[...].astype(jnp.float32)
        factor = lax.rsqrt(jnp.sum(values * values, axis=0, keepdims=True) + epsilon)
        turned_ref[part, :] = (values * factor).astype(jnp.bfloat16).T
        scale_ref[:, part] = factor


def unit_protos(at, blocks):
    rows, protos = blocks[0].shape
    width = rows * len(blocks)
    return pl.pallas_call(
        unit_protos_body,
        out_shape=(
            jax.ShapeDtypeStruct((protos, width), jnp.bfloat16),
            jax.ShapeDtypeStruct((1, protos), jnp.float32),
        ),
        in_specs=[SMEM] + [VMEM] * len(blocks),
        out_specs=(VMEM, VMEM),
        scratch_shapes=[pltpu.VMEM((width, min(512, protos)), jnp.bfloat16)],
        compiler_params=params(),
        name="unit_protos",
    )(at, *blocks)


def to_row(row_ref, tiles):
    for q in range(tiles.shape[0]):
        row_ref[:, q * 128 : (q + 1) * 128] = tiles[q : q + 1, :]


def to_tiles(tiles_ref, row_ref):
    for q in range(tiles_ref.shape[0]):
        tiles_ref[q : q + 1, :] = row_ref[:, q * 128 : (q + 1) * 128]


def received(got_ref, n):
    cores = []
    for core in range(CORES):
        total = got_ref[core, n]
        for device in range(core + CORES, got_ref.shape[0], CORES):
            total = total + got_ref[device, n]
        cores.append(total)
    return jnp.concatenate(cores, axis=0)


def sweep_body(gain, weigh, before, invert, turned_ref, unit_ref, *refs):
    if weigh:
        got_ref, *refs = refs
        if before:
            before_ref, *refs = refs
        sums_ref, crop_out, *refs = refs
        if invert:
            inv_ref, *refs = refs
        crop_row, total = refs
        crop = 1.0 / received(got_ref, 0)
        if before:
            crop = before_ref[...] * crop
        crop_out[...] = crop
        to_row(crop_row, crop)
    else:
        sums_ref, total = refs
    protos = turned_ref.shape[0]
    step = min(512, protos)
    total[...] = jnp.zeros_like(total)

    def block(i, carry):
        part = pl.ds(pl.multiple_of(i * step, step), step)
        mass = jnp.exp2(jnp.dot(turned_ref[part, :], unit_ref[...], preferred_element_type=jnp.float32) * gain)
        if weigh:
            mass = mass * crop_row[...]
        if gain == T_GAIN:
            inv = 1.0 / jnp.sum(mass, axis=1, keepdims=True)
            if invert:
                inv_ref[:, part] = inv.T
            mass = mass * inv
        total[...] += jnp.sum(mass.reshape(step // 8, 8, mass.shape[1]), axis=0)
        return carry

    lax.fori_loop(0, protos // step, block, 0)
    total[0:1, :] = jnp.sum(total[...], axis=0, keepdims=True)
    to_tiles(sums_ref, total.at[0:1, :])


def sweep(gain, turned, unit, got=None, before=None, invert=False):
    crops = unit.shape[1]
    tiles = jax.ShapeDtypeStruct((crops // 128, 128), jnp.float32)
    weigh = got is not None
    operands = [x for x in (turned, unit, got, before) if x is not None]
    out_shape = [tiles] + [tiles] * weigh
    if invert:
        out_shape.append(jax.ShapeDtypeStruct((1, turned.shape[0]), jnp.float32))
    row = pltpu.VMEM((1, crops), jnp.float32)
    return pl.pallas_call(
        functools.partial(sweep_body, gain, weigh, before is not None, invert),
        out_shape=out_shape,
        in_specs=[VMEM] * len(operands),
        out_specs=[VMEM] * len(out_shape),
        scratch_shapes=[row] * weigh + [pltpu.VMEM((8, crops), jnp.float32)],
        compiler_params=params(),
    )(*operands)


def grads_body(plan, at_ref, turned_ref, inv_ref, got_ref, both_ref, before_ref, *refs):
    nb, nz, rows, chunk, grain = plan
    teacher_ref, student_ref, crop_scale_ref, crop_out, by_proto, *refs = refs
    grad_ref, result, protos, inverse, crop_row, total_row, loss_sum = refs
    j, z, c = at_ref[0], at_ref[1], at_ref[2]
    count = turned_ref.shape[0]
    tile = student_ref.shape[1]
    step = pl.program_id(0)

    @pl.when(step == 0)
    def _():
        to_row(crop_row, jnp.log2(before_ref[...] / (received(got_ref, 0) * grain)))
        to_row(total_row, -jnp.log2(received(both_ref, 1) * grain))
        loss_sum[...] = jnp.zeros_like(loss_sum)
        for low in range(0, count, chunk):
            part = slice(low, low + chunk)
            protos[:, part] = turned_ref[part, :].T
            inverse[part, :] = jnp.broadcast_to(inv_ref[:, part], (128, chunk)).T
            by_proto[part, :] = jnp.zeros((chunk, by_proto.shape[1]), jnp.float32)

    inner = crop_row.shape[1] // nb // tile
    block, within = lax.div(step, inner), lax.rem(step, inner)
    here = pl.ds(pl.multiple_of(((j ^ block) * inner + within) * tile, tile), tile)
    loss = loss_sum[...]
    for low in range(0, count, chunk):
        part = slice(low, low + chunk)
        turned = turned_ref[part, :]
        by_teacher = jnp.dot(turned, teacher_ref[...], preferred_element_type=jnp.float32)
        by_student = jnp.dot(turned, student_ref[...], preferred_element_type=jnp.float32)
        inv = jnp.concatenate([inverse[part, :]] * (tile // 128), axis=1)
        targets = jnp.exp2(by_teacher * T_GAIN + crop_row[:, here]) * inv
        power = by_student * S_GAIN + total_row[:, here]
        grad_ref[part, :] = (jnp.exp2(power) - targets).astype(jnp.bfloat16)
        loss += jnp.sum((targets * power).reshape(chunk // 8, 8, tile), axis=0)
    loss_sum[...] = loss
    by_crop = jnp.dot(protos[...], grad_ref[...], preferred_element_type=jnp.float32)
    student = student_ref[...]
    values = student.astype(jnp.float32)
    radial = jnp.sum(values * by_crop, axis=0, keepdims=True)
    result[...] = (by_crop - values * radial) * crop_scale_ref[...]
    across = pl.ds(pl.multiple_of(within * tile, tile), tile)
    for oc in range(CORES):
        for oz in range(nz):
            top = pl.multiple_of(((z ^ oz) * CORES + (c ^ oc)) * rows, rows)
            target = pl.ds(pl.multiple_of((oz * nb + block) * rows, rows), rows)
            crop_out[oc, target, across] = result[pl.ds(top, rows), :]
    turned_student = student.T
    for low in range(0, count, chunk):
        part = slice(low, low + chunk)
        by_proto[part, :] += jnp.dot(grad_ref[part, :], turned_student, preferred_element_type=jnp.float32)

    @pl.when(step == pl.num_programs(0) - 1)
    def _():
        total = jnp.sum(jnp.sum(loss_sum[...], axis=0, keepdims=True), axis=1, keepdims=True)
        for oc in range(CORES):
            crop_out[oc, -8:, :] = jnp.broadcast_to(total, (8, crop_out.shape[2]))


def gradients(at, sizes, turned, inv, sums, teacher, student, crop_scale):
    nb, nz = sizes
    count, width = turned.shape
    crops = teacher.shape[1]
    rows, cols = width // (nz * CORES), crops // nb
    tile = min(256, cols)
    inner = cols // tile
    chunk = min(256, count)

    def across(height):
        return pl.BlockSpec((height, tile), lambda i, at_ref: (0, (at_ref[0] ^ (i // inner)) * inner + i % inner))

    fixed = [turned, inv] + list(sums)
    return pl.pallas_call(
        functools.partial(grads_body, (nb, nz, rows, chunk, crops * student_temp)),
        grid_spec=pltpu.PrefetchScalarGridSpec(
            num_scalar_prefetch=1,
            grid=(crops // tile,),
            in_specs=[VMEM] * len(fixed) + [across(width), across(width), across(1)],
            out_specs=[VMEM, VMEM],
            scratch_shapes=[
                pltpu.VMEM((count, tile), jnp.bfloat16),
                pltpu.VMEM((width, tile), jnp.float32),
                pltpu.VMEM((width, count), jnp.bfloat16),
                pltpu.VMEM((count, 128), jnp.float32),
                pltpu.VMEM((1, crops), jnp.float32),
                pltpu.VMEM((1, crops), jnp.float32),
                pltpu.VMEM((8, tile), jnp.float32),
            ],
        ),
        out_shape=[
            jax.ShapeDtypeStruct((CORES, nz * nb * rows + 8, cols), jnp.float32),
            jax.ShapeDtypeStruct((count, width), jnp.float32),
        ],
        compiler_params=params(),
        name="gradients",
    )(at, *fixed, teacher, student, crop_scale)


def finish_protos_body(nb, at_ref, by_proto, turned_ref, scale_ref, out_ref, top_ref, result):
    j = at_ref[0]
    count, width = by_proto.shape
    chunk = result.shape[1]
    wide = width // nb
    tops = jnp.zeros((1, chunk), jnp.float32)
    for low in range(0, count, chunk):
        part = slice(low, low + chunk)
        total = by_proto[part, :]
        values = turned_ref[part, :].astype(jnp.float32)
        radial = jnp.sum(values * total, axis=1, keepdims=True)
        final = (total - values * radial).T * scale_ref[:, part]
        result[...] = final
        tops = jnp.maximum(tops, jnp.max(jnp.abs(final), axis=0, keepdims=True))
        for o in range(nb):
            out_ref[o, :, part] = result[pl.ds(pl.multiple_of((j ^ o) * wide, wide), wide), :]
    top_ref[...] = jnp.broadcast_to(jnp.max(tops, axis=1, keepdims=True), top_ref.shape)


def finish_protos(at, nb, by_proto, turned, scale):
    count, width = turned.shape
    return pl.pallas_call(
        functools.partial(finish_protos_body, nb),
        out_shape=[
            jax.ShapeDtypeStruct((nb, width // nb, count), jnp.float32),
            jax.ShapeDtypeStruct((1, 128), jnp.float32),
        ],
        in_specs=[SMEM, VMEM, VMEM, VMEM],
        out_specs=[VMEM, VMEM],
        scratch_shapes=[pltpu.VMEM((width, min(256, count)), jnp.float32)],
        compiler_params=params(),
        name="finish_protos",
    )(at, by_proto, turned, scale)


def finish_crops_body(grain, crops, *refs):
    parts, (grad_ref, loss_ref) = refs[:-2], refs[-2:]
    total = parts[0][...]
    for ref in parts[1:]:
        total = total + ref[...]
    rows = grad_ref.shape[0]
    grad_ref[...] = total[:rows]
    loss_ref[...] = (total[rows : rows + 1, :128] * grain + math.log2(grain) * crops) * (-1.0 / (LOG2E * crops))


def finish_crops(parts, grain, crops):
    rows, cols = parts[0].shape
    return pl.pallas_call(
        functools.partial(finish_crops_body, grain, crops),
        out_shape=[
            jax.ShapeDtypeStruct((rows - 8, cols), jnp.float32),
            jax.ShapeDtypeStruct((1, 128), jnp.float32),
        ],
        in_specs=[VMEM] * len(parts),
        out_specs=[VMEM, VMEM],
        compiler_params=params(4),
        name="finish_crops",
    )(*parts)


def pack_body(at_ref, *refs):
    mine, theirs, out_ref = refs[: len(refs) // 2], refs[len(refs) // 2 : -1], refs[-1]
    half = out_ref.shape[2]
    part = pl.ds(pl.multiple_of(at_ref[2] * half, half), half)
    for n in range(len(mine)):
        total = mine[n][part, :] + theirs[n][part, :]
        for device in range(out_ref.shape[0]):
            out_ref[device, n] = total


def sum_everywhere(at, *tiles):
    devices = lax.axis_size("batch") * lax.axis_size("proto")
    theirs = [swap(x, 0, 0, 1) for x in tiles]
    sent = pl.pallas_call(
        pack_body,
        out_shape=jax.ShapeDtypeStruct((devices, len(tiles), tiles[0].shape[0] // CORES, 128), jnp.float32),
        in_specs=[SMEM] + [VMEM] * (2 * len(tiles)),
        out_specs=VMEM,
        compiler_params=params(),
        name="pack",
    )(at, *tiles, *theirs)
    return lax.all_to_all(sent, AXES, 0, 0)


def scatter_crops(parts, nz, nb, rows):
    kept = parts[0] + swap(parts[1], 0, 0, 1)
    extra = kept[nz * nb * rows :]
    kept = kept[: nz * nb * rows].reshape(nz, nb * rows, -1)
    masks = z_masks(nz)
    size = nb // 2 * rows
    held = [[kept[o, :size] for o in range(nz)], [kept[o, size:] for o in range(nz)]]
    for i in range(len(masks)):
        for side, order in enumerate((masks, masks[::-1])):
            span = [0]
            for later in order[i + 1 :]:
                span = span + [o ^ later for o in span]
            sent = [held[side][o ^ order[i]] for o in span] + [extra] * (side == 0)
            got = swap(jnp.concatenate(sent, axis=0), 0, order[i], 0)
            held[side] = {o: held[side][o] + got[n * size : (n + 1) * size] for n, o in enumerate(span)}
            if side == 0:
                more = extra + got[len(span) * size :]
        extra = more
    mine = [half[0][i * rows : (i + 1) * rows] for half in held for i in range(nb // 2)]
    return [jnp.concatenate([part, extra], axis=0) for part in mine]


def place_body(at_ref, *refs):
    parts, (out_ref, sems) = refs[:-2], refs[-2:]
    cols = parts[0].shape[1]
    copies = []
    for o, ref in enumerate(parts):
        left = pl.multiple_of((at_ref[0] ^ o) * cols, cols)
        copies.append(pltpu.make_async_copy(ref, out_ref.at[:, pl.ds(left, cols)], sems.at[o]))
        copies[-1].start()
    for copy in copies:
        copy.wait()


def place(at, parts):
    rows, cols = parts[0].shape
    return pl.pallas_call(
        place_body,
        out_shape=jax.ShapeDtypeStruct((rows, cols * len(parts)), jnp.float32),
        in_specs=[SMEM] + [VMEM] * len(parts),
        out_specs=pl.BlockSpec(memory_space=pl.ANY),
        scratch_shapes=[pltpu.SemaphoreType.DMA((len(parts),))],
        compiler_params=params(4),
        name="place",
    )(at, *parts)


def shards(teacher_emb, student_emb, prototypes):
    nb, nproto = lax.axis_size("batch"), lax.axis_size("proto")
    nz = nproto // CORES
    j, p = lax.axis_index("batch"), lax.axis_index("proto")
    at = jnp.stack([j, p // CORES, p % CORES]).astype(jnp.int32)
    width = teacher_emb.shape[0] * nproto
    crops = teacher_emb.shape[1] * nb
    count = prototypes.shape[1] // nb
    grain = crops * student_temp

    prototypes, at = lax.optimization_barrier((prototypes, at))

    def columns(o):
        return lax.dynamic_slice_in_dim(prototypes, (j ^ o) * count, count, 1)

    blocks = [columns(0)] + [swap(columns(o), o, 0, 0) for o in range(1, nb)]
    turned, proto_scale = unit_protos(at, blocks)
    teacher = unit_crops(at, gather_crops(teacher_emb), width, crops, 24)[0]
    student, crop_unit_scale = unit_crops(at, gather_crops(student_emb), width, crops, 60)

    (sums,) = sweep(T_GAIN, turned, teacher)
    got = sum_everywhere(at, sums)
    (softmax_sums,) = sweep(S_GAIN, turned, student)
    crop = None
    for iteration in range(1, ITERS):
        final = iteration == ITERS - 1
        sums, crop, *inv = sweep(T_GAIN, turned, teacher, got, crop, invert=final)
        got = sum_everywhere(at, sums, softmax_sums) if iteration == 1 else sum_everywhere(at, sums)
        both = got if iteration == 1 else both
    totals = (got, both, crop)
    crop_parts, by_proto = gradients(
        at, (nb, nz), turned, inv[0], totals, teacher, student, crop_unit_scale
    )
    mine = scatter_crops(crop_parts, nz, nb, teacher_emb.shape[0])
    proto_parts, top = finish_protos(at, nb, by_proto, turned, proto_scale)
    power = jnp.ceil(jnp.log2(jnp.maximum(top, 1e-30))) - 15.0
    edge = jnp.broadcast_to(power, (proto_parts.shape[1], 128))
    sent = [
        jnp.concatenate([proto_parts[o] * jnp.exp2(-power[:, :1]), edge], axis=1).astype(jnp.float16)
        for o in range(1, nb)
    ]
    got = [swap(x, o + 1, 0, 0).astype(jnp.float32) for o, x in enumerate(sent)]
    ready = [x[:, :count] * jnp.exp2(x[:1, count : count + 1]) for x in got]
    grad_proto = place(at, [proto_parts[0]] + ready)
    outs = [mine[0]] + [swap(mine[o], o, 0, 0) for o in range(1, nb)]
    grad_student, loss = finish_crops(outs, grain, crops)
    return (grad_proto, grad_student, loss[0, 0])


def solution(mesh):
    in_specs = (P("proto", "batch"), P("proto", "batch"), P("batch", "proto"))
    out_specs = (P("batch", "proto"), P("proto", "batch"), P())
    return jax.shard_map(shards, mesh=mesh, in_specs=in_specs, out_specs=out_specs, check_vma=False)
```

```python
import functools
import math

import jax
import jax.numpy as jnp
from jax import lax
from jax.experimental import pallas as pl
from jax.experimental.pallas import tpu as pltpu
from jax.sharding import PartitionSpec as P


ITERS = 3
CORES = 2
AXES = ("batch", "proto")

teacher_temp = 0.07
student_temp = 0.1
epsilon = 1e-06
LOG2E = 1.0 / math.log(2.0)
T_GAIN = LOG2E / teacher_temp
S_GAIN = LOG2E / student_temp

SMEM = pl.BlockSpec(memory_space=pltpu.SMEM)
VMEM = pl.BlockSpec(memory_space=pltpu.VMEM)


def params(megabytes=24):
    return pltpu.CompilerParams(vmem_limit_bytes=megabytes << 20)


def swap(x, over_batch, over_z, over_core):
    batch, proto = lax.axis_size("batch"), lax.axis_size("proto")
    pairs = []
    for b in range(batch):
        for p in range(proto):
            other = p ^ (over_z * CORES + over_core)
            pairs.append((b * proto + p, (b ^ over_batch) * proto + other))
    return lax.ppermute(x, AXES, pairs)


def z_masks(nz):
    return [1 << i for i in range(nz.bit_length() - 1)]


def join(parts, axis=1):
    return jnp.concatenate(parts, axis=axis)


def gather_crops(teacher, student):
    batch = lax.axis_size("batch")
    nz = lax.axis_size("proto") // CORES
    x = jnp.stack([teacher, student])[:, None]
    pieces = join([x] + [swap(x, o, 0, 0) for o in range(1, batch)])
    masks = z_masks(nz)
    held, offsets = [], []
    for first, order in ((0, masks), (batch // 2, masks[::-1])):
        now, plan = pieces[:, None, first : first + batch // 2], [0]
        for mask in order[:-1]:
            now = join([now, swap(now, 0, mask, 0)])
            plan = plan + [o ^ mask for o in plan]
        held.append(now)
        offsets.append(plan + [o ^ order[-1] for o in plan])
    found = []
    for which in range(2):
        both = []
        for side, mask in enumerate((masks[-1], masks[0])):
            half = held[side][which]
            half = join([half, swap(half, 0, mask, 0)], 0)
            first = side * (batch // 2)
            both.append((half, offsets[side], first, 0))
            both.append((swap(half, 0, 0, 1), offsets[side], first, 1))
        found.append(both)
    return found


def unit_crops_body(plan, at_ref, *refs):
    pieces, (unit_ref, scale_ref, raw, sems) = refs[: len(plan)], refs[len(plan) :]
    j, z, c = at_ref[0], at_ref[1], at_ref[2]
    copies = []
    for ref, (offsets, first, core) in zip(pieces, plan):
        rows, cols = ref.shape[2:]
        for i, oz in enumerate(offsets):
            top = pl.multiple_of(((z ^ oz) * CORES + (c ^ core)) * rows, rows)
            for k in range(ref.shape[1]):
                left = pl.multiple_of((j ^ (first + k)) * cols, cols)
                target = raw.at[pl.ds(top, rows), pl.ds(left, cols)]
                copies.append(pltpu.make_async_copy(ref.at[i, k], target, sems.at[len(copies)]))
                copies[-1].start()
    for copy in copies:
        copy.wait()
    for left in range(0, raw.shape[1], cols):
        part = slice(left, left + cols)
        values = raw[:, part].astype(jnp.float32)
        factor = lax.rsqrt(jnp.sum(values * values, axis=0, keepdims=True) + epsilon)
        unit_ref[:, part] = (values * factor).astype(jnp.bfloat16)
        scale_ref[:, part] = factor


def unit_crops(at, found, width, crops, megabytes):
    plan = [(offsets, first, core) for _, offsets, first, core in found]
    copies = sum(piece.shape[0] * piece.shape[1] for piece, *_ in found)
    return pl.pallas_call(
        functools.partial(unit_crops_body, plan),
        out_shape=(
            jax.ShapeDtypeStruct((width, crops), jnp.bfloat16),
            jax.ShapeDtypeStruct((1, crops), jnp.float32),
        ),
        in_specs=[SMEM] + [pl.BlockSpec(memory_space=pltpu.HBM)] * len(found),
        out_specs=(VMEM, VMEM),
        scratch_shapes=[
            pltpu.VMEM((width, crops), jnp.bfloat16),
            pltpu.SemaphoreType.DMA((copies,)),
        ],
        compiler_params=params(megabytes),
    )(at, *[piece for piece, *_ in found])


def unit_protos_body(at_ref, *refs):
    blocks, (turned_ref, scale_ref, raw) = refs[:-3], refs[-3:]
    j = at_ref[0]
    rows, step = blocks[0].shape[0], raw.shape[1]
    for low in range(0, blocks[0].shape[1], step):
        part = slice(low, low + step)
        for o, ref in enumerate(blocks):
            top = pl.multiple_of((j ^ o) * rows, rows)
            raw[pl.ds(top, rows), :] = ref[:, part]
        values = raw[...].astype(jnp.float32)
        factor = lax.rsqrt(jnp.sum(values * values, axis=0, keepdims=True) + epsilon)
        turned_ref[part, :] = (values * factor).astype(jnp.bfloat16).T
        scale_ref[:, part] = factor


def unit_protos(at, blocks):
    rows, protos = blocks[0].shape
    width = rows * len(blocks)
    return pl.pallas_call(
        unit_protos_body,
        out_shape=(
            jax.ShapeDtypeStruct((protos, width), jnp.bfloat16),
            jax.ShapeDtypeStruct((1, protos), jnp.float32),
        ),
        in_specs=[SMEM] + [VMEM] * len(blocks),
        out_specs=(VMEM, VMEM),
        scratch_shapes=[pltpu.VMEM((width, min(512, protos)), jnp.bfloat16)],
        compiler_params=params(),
        name="unit_protos",
    )(at, *blocks)


def to_row(row_ref, tiles):
    for q in range(tiles.shape[0]):
        row_ref[:, q * 128 : (q + 1) * 128] = tiles[q : q + 1, :]


def to_tiles(tiles_ref, row_ref):
    for q in range(tiles_ref.shape[0]):
        tiles_ref[q : q + 1, :] = row_ref[:, q * 128 : (q + 1) * 128]


def received(got_ref, n):
    cores = []
    for core in range(CORES):
        total = got_ref[core, n]
        for device in range(core + CORES, got_ref.shape[0], CORES):
            total = total + got_ref[device, n]
        cores.append(total)
    return jnp.concatenate(cores, axis=0)


def sweep_body(gain, weigh, before, invert, turned_ref, unit_ref, *refs):
    if weigh:
        got_ref, *refs = refs
        if before:
            before_ref, *refs = refs
        sums_ref, crop_out, *refs = refs
        if invert:
            inv_ref, *refs = refs
        crop_row, total = refs
        crop = 1.0 / received(got_ref, 0)
        if before:
            crop = before_ref[...] * crop
        crop_out[...] = crop
        to_row(crop_row, crop)
    else:
        sums_ref, total = refs
    protos = turned_ref.shape[0]
    step = min(512, protos)
    total[...] = jnp.zeros_like(total)

    def block(i, carry):
        part = pl.ds(pl.multiple_of(i * step, step), step)
        mass = jnp.exp2(jnp.dot(turned_ref[part, :], unit_ref[...], preferred_element_type=jnp.float32) * gain)
        if weigh:
            mass = mass * crop_row[...]
        if gain == T_GAIN:
            inv = 1.0 / jnp.sum(mass, axis=1, keepdims=True)
            if invert:
                inv_ref[:, part] = inv.T
            mass = mass * inv
        total[...] += jnp.sum(mass.reshape(step // 8, 8, mass.shape[1]), axis=0)
        return carry

    lax.fori_loop(0, protos // step, block, 0)
    total[0:1, :] = jnp.sum(total[...], axis=0, keepdims=True)
    to_tiles(sums_ref, total.at[0:1, :])


def sweep(gain, turned, unit, got=None, before=None, invert=False):
    crops = unit.shape[1]
    tiles = jax.ShapeDtypeStruct((crops // 128, 128), jnp.float32)
    weigh = got is not None
    operands = [x for x in (turned, unit, got, before) if x is not None]
    out_shape = [tiles] + [tiles] * weigh
    if invert:
        out_shape.append(jax.ShapeDtypeStruct((1, turned.shape[0]), jnp.float32))
    row = pltpu.VMEM((1, crops), jnp.float32)
    return pl.pallas_call(
        functools.partial(sweep_body, gain, weigh, before is not None, invert),
        out_shape=out_shape,
        in_specs=[VMEM] * len(operands),
        out_specs=[VMEM] * len(out_shape),
        scratch_shapes=[row] * weigh + [pltpu.VMEM((8, crops), jnp.float32)],
        compiler_params=params(),
    )(*operands)


def grads_body(plan, at_ref, turned_ref, inv_ref, got_ref, before_ref, *refs):
    nb, nz, rows, chunk, grain = plan
    teacher_ref, student_ref, crop_scale_ref, crop_out, by_proto, *refs = refs
    grad_ref, result, protos, inverse, crop_row, total_row, loss_sum = refs
    j, z, c = at_ref[0], at_ref[1], at_ref[2]
    count = turned_ref.shape[0]
    tile = student_ref.shape[1]
    step = pl.program_id(0)

    @pl.when(step == 0)
    def _():
        to_row(crop_row, jnp.log2(before_ref[...] / (received(got_ref, 0) * grain)))
        to_row(total_row, -jnp.log2(received(got_ref, 1) * grain))
        loss_sum[...] = jnp.zeros_like(loss_sum)
        for low in range(0, count, chunk):
            part = slice(low, low + chunk)
            protos[:, part] = turned_ref[part, :].T
            inverse[part, :] = jnp.broadcast_to(inv_ref[:, part], (128, chunk)).T
            by_proto[part, :] = jnp.zeros((chunk, by_proto.shape[1]), jnp.float32)

    inner = crop_row.shape[1] // nb // tile
    block, within = lax.div(step, inner), lax.rem(step, inner)
    here = pl.ds(pl.multiple_of(((j ^ block) * inner + within) * tile, tile), tile)
    loss = loss_sum[...]
    for low in range(0, count, chunk):
        part = slice(low, low + chunk)
        turned = turned_ref[part, :]
        by_teacher = jnp.dot(turned, teacher_ref[...], preferred_element_type=jnp.float32)
        by_student = jnp.dot(turned, student_ref[...], preferred_element_type=jnp.float32)
        inv = jnp.concatenate([inverse[part, :]] * (tile // 128), axis=1)
        targets = jnp.exp2(by_teacher * T_GAIN + crop_row[:, here]) * inv
        power = by_student * S_GAIN + total_row[:, here]
        grad_ref[part, :] = (jnp.exp2(power) - targets).astype(jnp.bfloat16)
        loss += jnp.sum((targets * power).reshape(chunk // 8, 8, tile), axis=0)
    loss_sum[...] = loss
    by_crop = jnp.dot(protos[...], grad_ref[...], preferred_element_type=jnp.float32)
    student = student_ref[...]
    values = student.astype(jnp.float32)
    radial = jnp.sum(values * by_crop, axis=0, keepdims=True)
    result[...] = (by_crop - values * radial) * crop_scale_ref[...]
    across = pl.ds(pl.multiple_of(within * tile, tile), tile)
    for oc in range(CORES):
        for oz in range(nz):
            top = pl.multiple_of(((z ^ oz) * CORES + (c ^ oc)) * rows, rows)
            target = pl.ds(pl.multiple_of((oz * nb + block) * rows, rows), rows)
            crop_out[oc, target, across] = result[pl.ds(top, rows), :]
    turned_student = student.T
    for low in range(0, count, chunk):
        part = slice(low, low + chunk)
        by_proto[part, :] += jnp.dot(grad_ref[part, :], turned_student, preferred_element_type=jnp.float32)

    @pl.when(step == pl.num_programs(0) - 1)
    def _():
        total = jnp.sum(jnp.sum(loss_sum[...], axis=0, keepdims=True), axis=1, keepdims=True)
        for oc in range(CORES):
            crop_out[oc, -8:, :] = jnp.broadcast_to(total, (8, crop_out.shape[2]))


def gradients(at, sizes, turned, inv, got, before, teacher, student, crop_scale):
    nb, nz = sizes
    count, width = turned.shape
    crops = teacher.shape[1]
    rows, cols = width // (nz * CORES), crops // nb
    tile = min(256, cols)
    inner = cols // tile
    chunk = min(256, count)

    def across(height):
        return pl.BlockSpec((height, tile), lambda i, at_ref: (0, (at_ref[0] ^ (i // inner)) * inner + i % inner))

    fixed = [turned, inv, got, before]
    return pl.pallas_call(
        functools.partial(grads_body, (nb, nz, rows, chunk, crops * student_temp)),
        grid_spec=pltpu.PrefetchScalarGridSpec(
            num_scalar_prefetch=1,
            grid=(crops // tile,),
            in_specs=[VMEM] * len(fixed) + [across(width), across(width), across(1)],
            out_specs=[VMEM, VMEM],
            scratch_shapes=[
                pltpu.VMEM((count, tile), jnp.bfloat16),
                pltpu.VMEM((width, tile), jnp.float32),
                pltpu.VMEM((width, count), jnp.bfloat16),
                pltpu.VMEM((count, 128), jnp.float32),
                pltpu.VMEM((1, crops), jnp.float32),
                pltpu.VMEM((1, crops), jnp.float32),
                pltpu.VMEM((8, tile), jnp.float32),
            ],
        ),
        out_shape=[
            jax.ShapeDtypeStruct((CORES, nz * nb * rows + 8, cols), jnp.float32),
            jax.ShapeDtypeStruct((count, width), jnp.float32),
        ],
        compiler_params=params(),
        name="gradients",
    )(at, *fixed, teacher, student, crop_scale)


def finish_protos_body(nb, at_ref, by_proto, turned_ref, scale_ref, out_ref, top_ref, result):
    j = at_ref[0]
    count, width = by_proto.shape
    chunk = result.shape[1]
    wide = width // nb
    tops = jnp.zeros((1, chunk), jnp.float32)
    for low in range(0, count, chunk):
        part = slice(low, low + chunk)
        total = by_proto[part, :]
        values = turned_ref[part, :].astype(jnp.float32)
        radial = jnp.sum(values * total, axis=1, keepdims=True)
        final = (total - values * radial).T * scale_ref[:, part]
        result[...] = final
        tops = jnp.maximum(tops, jnp.max(jnp.abs(final), axis=0, keepdims=True))
        for o in range(nb):
            out_ref[o, :, part] = result[pl.ds(pl.multiple_of((j ^ o) * wide, wide), wide), :]
    top_ref[...] = jnp.broadcast_to(jnp.max(tops, axis=1, keepdims=True), top_ref.shape)


def finish_protos(at, nb, by_proto, turned, scale):
    count, width = turned.shape
    return pl.pallas_call(
        functools.partial(finish_protos_body, nb),
        out_shape=[
            jax.ShapeDtypeStruct((nb, width // nb, count), jnp.float32),
            jax.ShapeDtypeStruct((1, 128), jnp.float32),
        ],
        in_specs=[SMEM, VMEM, VMEM, VMEM],
        out_specs=[VMEM, VMEM],
        scratch_shapes=[pltpu.VMEM((width, min(256, count)), jnp.float32)],
        compiler_params=params(),
        name="finish_protos",
    )(at, by_proto, turned, scale)


def finish_crops_body(grain, crops, *refs):
    parts, (grad_ref, loss_ref) = refs[:-2], refs[-2:]
    total = parts[0][...]
    for ref in parts[1:]:
        total = total + ref[...]
    rows = grad_ref.shape[0]
    grad_ref[...] = total[:rows]
    loss_ref[...] = (total[rows : rows + 1, :128] * grain + math.log2(grain) * crops) * (-1.0 / (LOG2E * crops))


def finish_crops(parts, grain, crops):
    rows, cols = parts[0].shape
    return pl.pallas_call(
        functools.partial(finish_crops_body, grain, crops),
        out_shape=[
            jax.ShapeDtypeStruct((rows - 8, cols), jnp.float32),
            jax.ShapeDtypeStruct((1, 128), jnp.float32),
        ],
        in_specs=[VMEM] * len(parts),
        out_specs=[VMEM, VMEM],
        compiler_params=params(4),
        name="finish_crops",
    )(*parts)


def pack_body(at_ref, *refs):
    mine, theirs, out_ref = refs[: len(refs) // 2], refs[len(refs) // 2 : -1], refs[-1]
    half = out_ref.shape[2]
    part = pl.ds(pl.multiple_of(at_ref[2] * half, half), half)
    for n in range(len(mine)):
        total = mine[n][part, :] + theirs[n][part, :]
        for device in range(out_ref.shape[0]):
            out_ref[device, n] = total


def sum_everywhere(at, *tiles):
    devices = lax.axis_size("batch") * lax.axis_size("proto")
    theirs = [swap(x, 0, 0, 1) for x in tiles]
    sent = pl.pallas_call(
        pack_body,
        out_shape=jax.ShapeDtypeStruct((devices, len(tiles), tiles[0].shape[0] // CORES, 128), jnp.float32),
        in_specs=[SMEM] + [VMEM] * (2 * len(tiles)),
        out_specs=VMEM,
        compiler_params=params(),
        name="pack",
    )(at, *tiles, *theirs)
    return lax.all_to_all(sent, AXES, 0, 0)


def scatter_crops(parts, nz, nb, rows):
    kept = parts[0] + swap(parts[1], 0, 0, 1)
    extra = kept[nz * nb * rows :]
    kept = kept[: nz * nb * rows].reshape(nz, nb * rows, -1)
    masks = z_masks(nz)
    size = nb // 2 * rows
    held = [[kept[o, :size] for o in range(nz)], [kept[o, size:] for o in range(nz)]]
    for i in range(len(masks)):
        for side, order in enumerate((masks, masks[::-1])):
            span = [0]
            for later in order[i + 1 :]:
                span = span + [o ^ later for o in span]
            sent = [held[side][o ^ order[i]] for o in span] + [extra] * (side == 0)
            got = swap(jnp.concatenate(sent, axis=0), 0, order[i], 0)
            held[side] = {o: held[side][o] + got[n * size : (n + 1) * size] for n, o in enumerate(span)}
            if side == 0:
                more = extra + got[len(span) * size :]
            if i < len(masks) - 1:
                held[side] = lax.optimization_barrier(held[side])
        extra = more
    mine = [half[0][i * rows : (i + 1) * rows] for half in held for i in range(nb // 2)]
    return [jnp.concatenate([part, extra], axis=0) for part in mine]


def place_body(at_ref, *refs):
    parts, (out_ref, scaled, sems) = refs[:-3], refs[-3:]
    cols = parts[0].shape[1]
    copies = []
    for o, ref in enumerate(parts):
        left = pl.multiple_of((at_ref[0] ^ o) * cols, cols)
        source = ref
        if o:
            source = scaled.at[o - 1]
            gain = jnp.exp2(ref[:, cols:])
            source[...] = ref[:, :cols] * jnp.concatenate([gain] * (cols // 128), axis=1)
        copies.append(pltpu.make_async_copy(source, out_ref.at[:, pl.ds(left, cols)], sems.at[o]))
        copies[-1].start()
    for copy in copies:
        copy.wait()


def place(at, parts):
    rows, cols = parts[0].shape
    return pl.pallas_call(
        place_body,
        out_shape=jax.ShapeDtypeStruct((rows, cols * len(parts)), jnp.float32),
        in_specs=[SMEM] + [VMEM] * len(parts),
        out_specs=pl.BlockSpec(memory_space=pl.ANY),
        scratch_shapes=[
            pltpu.VMEM((len(parts) - 1, rows, cols), jnp.float32),
            pltpu.SemaphoreType.DMA((len(parts),)),
        ],
        compiler_params=params(16),
        name="place",
    )(at, *parts)


def shards(teacher_emb, student_emb, prototypes):
    nb, nproto = lax.axis_size("batch"), lax.axis_size("proto")
    nz = nproto // CORES
    j, p = lax.axis_index("batch"), lax.axis_index("proto")
    at = jnp.stack([j, p // CORES, p % CORES]).astype(jnp.int32)
    width = teacher_emb.shape[0] * nproto
    crops = teacher_emb.shape[1] * nb
    count = prototypes.shape[1] // nb
    grain = crops * student_temp

    prototypes, at = lax.optimization_barrier((prototypes, at))

    def columns(o):
        return lax.dynamic_slice_in_dim(prototypes, (j ^ o) * count, count, 1)

    blocks = [columns(0)] + [swap(columns(o), o, 0, 0) for o in range(1, nb)]
    turned, proto_scale = unit_protos(at, blocks)
    found = gather_crops(teacher_emb, student_emb)
    teacher = unit_crops(at, found[0], width, crops, 24)[0]
    student, crop_unit_scale = unit_crops(at, found[1], width, crops, 60)

    (sums,) = sweep(T_GAIN, turned, teacher)
    got, crop, inv = sum_everywhere(at, sums), None, []
    for iteration in range(1, ITERS):
        final = iteration == ITERS - 1
        sums, crop, *inv = sweep(T_GAIN, turned, teacher, got, crop, invert=final)
        if final:
            got = sum_everywhere(at, sums, softmax_total)
        else:
            got = sum_everywhere(at, sums)
            (softmax_total,) = sweep(S_GAIN, turned, student)
    crop_parts, by_proto = gradients(at, (nb, nz), turned, inv[0], got, crop, teacher, student, crop_unit_scale)
    mine = scatter_crops(crop_parts, nz, nb, teacher_emb.shape[0])
    proto_parts, top = finish_protos(at, nb, by_proto, turned, proto_scale)
    power = jnp.ceil(jnp.log2(jnp.maximum(top, 1e-30))) - 15.0
    edge = jnp.broadcast_to(power, (proto_parts.shape[1], 128))
    sent = [
        jnp.concatenate([proto_parts[o] * jnp.exp2(-power[:, :1]), edge], axis=1).astype(jnp.float16)
        for o in range(1, nb)
    ]
    got = [swap(x, o + 1, 0, 0) for o, x in enumerate(sent)]
    got, mine = lax.optimization_barrier((got, mine))
    ready = [x.astype(jnp.float32) for x in got]
    grad_proto = place(at, [proto_parts[0]] + ready)
    outs = [mine[0]] + [swap(mine[o], o, 0, 0) for o in range(1, nb)]
    grad_student, loss = finish_crops(outs, grain, crops)
    return (grad_proto, grad_student, loss[0, 0])


def solution(mesh):
    in_specs = (P("proto", "batch"), P("proto", "batch"), P("batch", "proto"))
    out_specs = (P("batch", "proto"), P("proto", "batch"), P())
    return jax.shard_map(shards, mesh=mesh, in_specs=in_specs, out_specs=out_specs, check_vma=False)
```

```python
import functools
import math

import jax
import jax.numpy as jnp
from jax import lax
from jax.experimental import pallas as pl
from jax.experimental.pallas import tpu as pltpu
from jax.sharding import PartitionSpec as P


ITERS = 3
CORES = 2
AXES = ("batch", "proto")

teacher_temp = 0.07
student_temp = 0.1
epsilon = 1e-06
LOG2E = 1.0 / math.log(2.0)
T_GAIN = LOG2E / teacher_temp
S_GAIN = LOG2E / student_temp

SMEM = pl.BlockSpec(memory_space=pltpu.SMEM)
VMEM = pl.BlockSpec(memory_space=pltpu.VMEM)


def params(megabytes=24):
    return pltpu.CompilerParams(vmem_limit_bytes=megabytes << 20)


def swap(x, over_batch, over_z, over_core):
    batch, proto = lax.axis_size("batch"), lax.axis_size("proto")
    pairs = []
    for b in range(batch):
        for p in range(proto):
            other = p ^ (over_z * CORES + over_core)
            pairs.append((b * proto + p, (b ^ over_batch) * proto + other))
    return lax.ppermute(x, AXES, pairs)


def z_masks(nz):
    return [1 << i for i in range(nz.bit_length() - 1)]


def join(parts):
    return jnp.concatenate(parts, axis=0)


def gather_crops(teacher, student):
    batch = lax.axis_size("batch")
    nz = lax.axis_size("proto") // CORES
    both = jnp.stack([teacher, student])
    passed = [both] + [swap(both, 0, o, 0) for o in range(1, nz)]
    found = []
    for which in range(2):
        mine = join([x[which][None] for x in passed])[None]
        pieces = join([mine] + [swap(mine, o, 0, 0) for o in range(1, batch)])
        found.append([pieces, swap(pieces, 0, 0, 1)])
    return found


def unit_crops_body(at_ref, *refs):
    pieces, (unit_ref, scale_ref, raw, sems) = refs[:CORES], refs[CORES:]
    j, z, c = at_ref[0], at_ref[1], at_ref[2]
    copies = []
    for core, ref in enumerate(pieces):
        batch, nz, rows, cols = ref.shape
        for ob in range(batch):
            left = pl.multiple_of((j ^ ob) * cols, cols)
            for oz in range(nz):
                top = pl.multiple_of(((z ^ oz) * CORES + (c ^ core)) * rows, rows)
                target = raw.at[pl.ds(top, rows), pl.ds(left, cols)]
                copies.append(pltpu.make_async_copy(ref.at[ob, oz], target, sems.at[len(copies)]))
                copies[-1].start()
    for copy in copies:
        copy.wait()
    for left in range(0, raw.shape[1], cols):
        part = slice(left, left + cols)
        values = raw[:, part].astype(jnp.float32)
        factor = lax.rsqrt(jnp.sum(values * values, axis=0, keepdims=True) + epsilon)
        unit_ref[:, part] = (values * factor).astype(jnp.bfloat16)
        scale_ref[:, part] = factor


def unit_crops(at, found, width, crops, megabytes):
    copies = CORES * found[0].shape[0] * found[0].shape[1]
    return pl.pallas_call(
        unit_crops_body,
        out_shape=(
            jax.ShapeDtypeStruct((width, crops), jnp.bfloat16),
            jax.ShapeDtypeStruct((1, crops), jnp.float32),
        ),
        in_specs=[SMEM] + [pl.BlockSpec(memory_space=pltpu.HBM)] * len(found),
        out_specs=(VMEM, VMEM),
        scratch_shapes=[
            pltpu.VMEM((width, crops), jnp.bfloat16),
            pltpu.SemaphoreType.DMA((copies,)),
        ],
        compiler_params=params(megabytes),
    )(at, *found)


def unit_protos_body(at_ref, *refs):
    blocks, (turned_ref, scale_ref, raw) = refs[:-3], refs[-3:]
    j = at_ref[0]
    rows, step = blocks[0].shape[0], raw.shape[1]
    for low in range(0, blocks[0].shape[1], step):
        part = slice(low, low + step)
        for o, ref in enumerate(blocks):
            top = pl.multiple_of((j ^ o) * rows, rows)
            raw[pl.ds(top, rows), :] = ref[:, part]
        values = raw[...].astype(jnp.float32)
        factor = lax.rsqrt(jnp.sum(values * values, axis=0, keepdims=True) + epsilon)
        turned_ref[part, :] = (values * factor).astype(jnp.bfloat16).T
        scale_ref[:, part] = factor


def unit_protos(at, blocks):
    rows, protos = blocks[0].shape
    width = rows * len(blocks)
    return pl.pallas_call(
        unit_protos_body,
        out_shape=(
            jax.ShapeDtypeStruct((protos, width), jnp.bfloat16),
            jax.ShapeDtypeStruct((1, protos), jnp.float32),
        ),
        in_specs=[SMEM] + [VMEM] * len(blocks),
        out_specs=(VMEM, VMEM),
        scratch_shapes=[pltpu.VMEM((width, min(512, protos)), jnp.bfloat16)],
        compiler_params=params(),
        name="unit_protos",
    )(at, *blocks)


def to_row(row_ref, tiles):
    for q in range(tiles.shape[0]):
        row_ref[:, q * 128 : (q + 1) * 128] = tiles[q : q + 1, :]


def to_tiles(tiles_ref, row_ref):
    for q in range(tiles_ref.shape[0]):
        tiles_ref[q : q + 1, :] = row_ref[:, q * 128 : (q + 1) * 128]


def received(got_ref, n):
    cores = []
    for core in range(CORES):
        total = got_ref[core, n]
        for device in range(core + CORES, got_ref.shape[0], CORES):
            total = total + got_ref[device, n]
        cores.append(total)
    return jnp.concatenate(cores, axis=0)


def sweep_body(gain, weigh, before, invert, turned_ref, unit_ref, *refs):
    if weigh:
        got_ref, *refs = refs
        if before:
            before_ref, *refs = refs
        sums_ref, crop_out, *refs = refs
        if invert:
            inv_ref, *refs = refs
        crop_row, total = refs
        crop = 1.0 / received(got_ref, 0)
        if before:
            crop = before_ref[...] * crop
        crop_out[...] = crop
        to_row(crop_row, crop)
    else:
        sums_ref, total = refs
    protos = turned_ref.shape[0]
    step = min(512, protos)
    total[...] = jnp.zeros_like(total)

    def block(i, carry):
        part = pl.ds(pl.multiple_of(i * step, step), step)
        mass = jnp.exp2(jnp.dot(turned_ref[part, :], unit_ref[...], preferred_element_type=jnp.float32) * gain)
        if weigh:
            mass = mass * crop_row[...]
        if gain == T_GAIN:
            inv = 1.0 / jnp.sum(mass, axis=1, keepdims=True)
            if invert:
                inv_ref[:, part] = inv.T
            mass = mass * inv
        total[...] += jnp.sum(mass.reshape(step // 8, 8, mass.shape[1]), axis=0)
        return carry

    lax.fori_loop(0, protos // step, block, 0)
    total[0:1, :] = jnp.sum(total[...], axis=0, keepdims=True)
    to_tiles(sums_ref, total.at[0:1, :])


def sweep(gain, turned, unit, got=None, before=None, invert=False):
    crops = unit.shape[1]
    tiles = jax.ShapeDtypeStruct((crops // 128, 128), jnp.float32)
    weigh = got is not None
    operands = [x for x in (turned, unit, got, before) if x is not None]
    out_shape = [tiles] + [tiles] * weigh
    if invert:
        out_shape.append(jax.ShapeDtypeStruct((1, turned.shape[0]), jnp.float32))
    row = pltpu.VMEM((1, crops), jnp.float32)
    return pl.pallas_call(
        functools.partial(sweep_body, gain, weigh, before is not None, invert),
        out_shape=out_shape,
        in_specs=[VMEM] * len(operands),
        out_specs=[VMEM] * len(out_shape),
        scratch_shapes=[row] * weigh + [pltpu.VMEM((8, crops), jnp.float32)],
        compiler_params=params(),
    )(*operands)


def prepare_body(grain, turned_ref, inv_ref, got_ref, before_ref, protos, inverse, crop_row, total_row):
    to_row(crop_row, jnp.log2(before_ref[...] / (received(got_ref, 0) * grain)))
    to_row(total_row, -jnp.log2(received(got_ref, 1) * grain))
    count = turned_ref.shape[0]
    chunk = min(256, count)
    for low in range(0, count, chunk):
        part = slice(low, low + chunk)
        protos[:, part] = turned_ref[part, :].T
        inverse[part, :] = jnp.broadcast_to(inv_ref[:, part], (128, chunk)).T


def prepare(turned, inv, got, before, grain):
    count, width = turned.shape
    crops = before.shape[0] * 128
    return pl.pallas_call(
        functools.partial(prepare_body, grain),
        out_shape=[
            jax.ShapeDtypeStruct((width, count), jnp.bfloat16),
            jax.ShapeDtypeStruct((count, 128), jnp.float32),
            jax.ShapeDtypeStruct((1, crops), jnp.float32),
            jax.ShapeDtypeStruct((1, crops), jnp.float32),
        ],
        in_specs=[VMEM] * 4,
        out_specs=[VMEM] * 4,
        compiler_params=params(16),
        name="prepare",
    )(turned, inv, got, before)


def grads_body(plan, at_ref, turned_ref, protos_ref, inverse_ref, *refs):
    nz, first, blocks, rows, chunk, tile, end = plan
    if first:
        before_ref, loss_before_ref, *refs = refs
    crop_ref, total_ref, teacher_ref, student_ref, crop_scale_ref, crop_out, by_proto, loss_sum, grad_ref, result = refs
    j, z, c = at_ref[0], at_ref[1], at_ref[2]
    count = turned_ref.shape[0]
    cols = crop_out.shape[2]
    loss = loss_before_ref[...] if first else jnp.zeros_like(loss_sum)
    for step in range(blocks * cols // tile):
        block, within = divmod(step * tile, cols)
        here = pl.ds(pl.multiple_of((j ^ (first + block)) * cols + within, tile), tile)
        teacher, student = teacher_ref[:, here], student_ref[:, here]
        crop, total = crop_ref[:, here], total_ref[:, here]
        grads = grad_ref.at[step % 2]
        for low in range(0, count, chunk):
            part = slice(low, low + chunk)
            turned = turned_ref[part, :]
            by_teacher = jnp.dot(turned, teacher, preferred_element_type=jnp.float32)
            by_student = jnp.dot(turned, student, preferred_element_type=jnp.float32)
            inv = jnp.concatenate([inverse_ref[part, :]] * (tile // 128), axis=1)
            targets = jnp.exp2(by_teacher * T_GAIN + crop) * inv
            power = by_student * S_GAIN + total
            grads[part, :] = (jnp.exp2(power) - targets).astype(jnp.bfloat16)
            loss += jnp.sum((targets * power).reshape(chunk // 8, 8, tile), axis=0)
        by_crop = jnp.dot(protos_ref[...], grads[...], preferred_element_type=jnp.float32)
        values = student.astype(jnp.float32)
        radial = jnp.sum(values * by_crop, axis=0, keepdims=True)
        result[step % 2] = (by_crop - values * radial) * crop_scale_ref[:, here]
        for oc in range(CORES):
            for oz in range(nz):
                top = pl.multiple_of(((z ^ oz) * CORES + (c ^ oc)) * rows, rows)
                low = (oz * blocks + block) * rows
                crop_out[oc, low : low + rows, within : within + tile] = result[step % 2, pl.ds(top, rows), :]
        turned_student = student.T
        for low in range(0, count, chunk):
            part = slice(low, low + chunk)
            more = jnp.dot(grads[part, :], turned_student, preferred_element_type=jnp.float32)
            old = by_proto if step else before_ref if first else None
            by_proto[part, :] = more if old is None else old[part, :] + more
    loss_sum[...] = loss
    if end:
        total = jnp.sum(jnp.sum(loss, axis=0, keepdims=True), axis=1, keepdims=True)
        for oc in range(CORES):
            crop_out[oc, -8:, :] = jnp.broadcast_to(total, (8, cols))


def gradients(at, sizes, group, groups, turned, prepared, sums, teacher, student, crop_scale):
    nb, nz = sizes
    count, width = turned.shape
    crops = teacher.shape[1]
    rows, cols = width // (nz * CORES), crops // nb
    blocks = nb // groups
    tile = min(256, cols)
    chunk = min(256, count)
    end = group == groups - 1
    protos, inverse, crop_row, total_row = prepared
    operands = [turned, protos, inverse] + list(sums) + [crop_row, total_row, teacher, student, crop_scale]
    return pl.pallas_call(
        functools.partial(grads_body, (nz, group * blocks, blocks, rows, chunk, tile, end)),
        in_specs=[SMEM] + [VMEM] * len(operands),
        out_specs=[VMEM, VMEM, VMEM],
        scratch_shapes=[
            pltpu.VMEM((2, count, tile), jnp.bfloat16),
            pltpu.VMEM((2, width, tile), jnp.float32),
        ],
        out_shape=[
            jax.ShapeDtypeStruct((CORES, nz * blocks * rows + 8 * end, cols), jnp.float32),
            jax.ShapeDtypeStruct((count, width), jnp.float32),
            jax.ShapeDtypeStruct((8, tile), jnp.float32),
        ],
        compiler_params=params(20),
    )(at, *operands)


def finish_protos_body(nb, at_ref, by_proto, turned_ref, scale_ref, out_ref, top_ref, result):
    j = at_ref[0]
    count, width = by_proto.shape
    chunk = result.shape[1]
    wide = width // nb
    tops = jnp.zeros((1, chunk), jnp.float32)
    for low in range(0, count, chunk):
        part = slice(low, low + chunk)
        total = by_proto[part, :]
        values = turned_ref[part, :].astype(jnp.float32)
        radial = jnp.sum(values * total, axis=1, keepdims=True)
        final = (total - values * radial).T * scale_ref[:, part]
        result[...] = final
        tops = jnp.maximum(tops, jnp.max(jnp.abs(final), axis=0, keepdims=True))
        for o in range(nb):
            out_ref[o, :, part] = result[pl.ds(pl.multiple_of((j ^ o) * wide, wide), wide), :]
    top_ref[...] = jnp.broadcast_to(jnp.max(tops, axis=1, keepdims=True), top_ref.shape)


def finish_protos(at, nb, by_proto, turned, scale):
    count, width = turned.shape
    return pl.pallas_call(
        functools.partial(finish_protos_body, nb),
        out_shape=[
            jax.ShapeDtypeStruct((nb, width // nb, count), jnp.float32),
            jax.ShapeDtypeStruct((1, 128), jnp.float32),
        ],
        in_specs=[SMEM, VMEM, VMEM, VMEM],
        out_specs=[VMEM, VMEM],
        scratch_shapes=[pltpu.VMEM((width, min(256, count)), jnp.float32)],
        compiler_params=params(),
        name="finish_protos",
    )(at, by_proto, turned, scale)


def finish_crops_body(grain, crops, *refs):
    parts, (grad_ref, loss_ref) = refs[:-2], refs[-2:]
    total = parts[0][...]
    for ref in parts[1:]:
        total = total + ref[...]
    rows = grad_ref.shape[0]
    grad_ref[...] = total[:rows]
    loss_ref[...] = (total[rows : rows + 1, :128] * grain + math.log2(grain) * crops) * (-1.0 / (LOG2E * crops))


def finish_crops(parts, grain, crops):
    rows, cols = parts[0].shape
    return pl.pallas_call(
        functools.partial(finish_crops_body, grain, crops),
        out_shape=[
            jax.ShapeDtypeStruct((rows - 8, cols), jnp.float32),
            jax.ShapeDtypeStruct((1, 128), jnp.float32),
        ],
        in_specs=[VMEM] * len(parts),
        out_specs=[VMEM, VMEM],
        compiler_params=params(4),
        name="finish_crops",
    )(*parts)


def pack_body(at_ref, *refs):
    mine, theirs, out_ref = refs[: len(refs) // 2], refs[len(refs) // 2 : -1], refs[-1]
    half = out_ref.shape[2]
    part = pl.ds(pl.multiple_of(at_ref[2] * half, half), half)
    for n in range(len(mine)):
        total = mine[n][part, :] + theirs[n][part, :]
        for device in range(out_ref.shape[0]):
            out_ref[device, n] = total


def sum_everywhere(at, *tiles):
    devices = lax.axis_size("batch") * lax.axis_size("proto")
    theirs = [swap(x, 0, 0, 1) for x in tiles]
    sent = pl.pallas_call(
        pack_body,
        out_shape=jax.ShapeDtypeStruct((devices, len(tiles), tiles[0].shape[0] // CORES, 128), jnp.float32),
        in_specs=[SMEM] + [VMEM] * (2 * len(tiles)),
        out_specs=VMEM,
        compiler_params=params(),
        name="pack",
    )(at, *tiles, *theirs)
    return lax.all_to_all(sent, AXES, 0, 0)


def scatter_crops(parts, nz, rows):
    kept = parts[0] + swap(parts[1], 0, 0, 1)
    blocks = kept.shape[0] // (nz * rows)
    size = blocks * rows
    extra = kept[nz * size :]
    held = {o: kept[o * size : (o + 1) * size] for o in range(nz)}
    masks = z_masks(nz)
    for i, mask in enumerate(masks):
        span = [0]
        for later in masks[i + 1 :]:
            span = span + [o ^ later for o in span]
        sent = [held[o ^ mask] for o in span] + [extra] * bool(extra.shape[0])
        got = swap(jnp.concatenate(sent, axis=0), 0, mask, 0)
        held = {o: held[o] + got[n * size : (n + 1) * size] for n, o in enumerate(span)}
        extra = extra + got[len(span) * size :]
        held, extra = lax.optimization_barrier((held, extra))
    return [held[0][i * rows : (i + 1) * rows] for i in range(blocks)], extra


def place_body(at_ref, *refs):
    parts, (out_ref, scaled, sems) = refs[:-3], refs[-3:]
    cols = parts[0].shape[1]
    copies = []
    for o, ref in enumerate(parts):
        left = pl.multiple_of((at_ref[0] ^ o) * cols, cols)
        source = ref
        if o:
            source = scaled.at[o - 1]
            gain = jnp.exp2(ref[:, cols:])
            source[...] = ref[:, :cols] * jnp.concatenate([gain] * (cols // 128), axis=1)
        copies.append(pltpu.make_async_copy(source, out_ref.at[:, pl.ds(left, cols)], sems.at[o]))
        copies[-1].start()
    for copy in copies:
        copy.wait()


def place(at, parts):
    rows, cols = parts[0].shape
    return pl.pallas_call(
        place_body,
        out_shape=jax.ShapeDtypeStruct((rows, cols * len(parts)), jnp.float32),
        in_specs=[SMEM] + [VMEM] * len(parts),
        out_specs=pl.BlockSpec(memory_space=pl.ANY),
        scratch_shapes=[
            pltpu.VMEM((len(parts) - 1, rows, cols), jnp.float32),
            pltpu.SemaphoreType.DMA((len(parts),)),
        ],
        compiler_params=params(16),
        name="place",
    )(at, *parts)


def shards(teacher_emb, student_emb, prototypes):
    nb, nproto = lax.axis_size("batch"), lax.axis_size("proto")
    nz = nproto // CORES
    j, p = lax.axis_index("batch"), lax.axis_index("proto")
    at = jnp.stack([j, p // CORES, p % CORES]).astype(jnp.int32)
    width = teacher_emb.shape[0] * nproto
    crops = teacher_emb.shape[1] * nb
    count = prototypes.shape[1] // nb
    grain = crops * student_temp

    prototypes, at = lax.optimization_barrier((prototypes, at))

    def columns(o):
        return lax.dynamic_slice_in_dim(prototypes, (j ^ o) * count, count, 1)

    blocks = [columns(0)] + [swap(columns(o), o, 0, 0) for o in range(1, nb)]
    turned, proto_scale = unit_protos(at, blocks)
    found = gather_crops(teacher_emb, student_emb)
    teacher = unit_crops(at, found[0], width, crops, 24)[0]
    student, crop_unit_scale = unit_crops(at, found[1], width, crops, 60)

    (sums,) = sweep(T_GAIN, turned, teacher)
    got, crop, inv = sum_everywhere(at, sums), None, []
    for iteration in range(1, ITERS):
        final = iteration == ITERS - 1
        sums, crop, *inv = sweep(T_GAIN, turned, teacher, got, crop, invert=final)
        if final:
            got = sum_everywhere(at, sums, softmax_total)
        else:
            got = sum_everywhere(at, sums)
            (softmax_total,) = sweep(S_GAIN, turned, student)
    prepared = prepare(turned, inv[0], got, crop, grain)
    groups = min(4, nb)
    mine, sums = [], []
    for group in range(groups):
        crop_parts, *sums = gradients(
            at, (nb, nz), group, groups, turned, prepared, sums, teacher, student, crop_unit_scale
        )
        more, extra = scatter_crops(crop_parts, nz, teacher_emb.shape[0])
        mine += more
    by_proto = sums[0]
    mine = [jnp.concatenate([part, extra], axis=0) for part in mine]
    proto_parts, top = finish_protos(at, nb, by_proto, turned, proto_scale)
    power = jnp.ceil(jnp.log2(jnp.maximum(top, 1e-30))) - 15.0
    edge = jnp.broadcast_to(power, (proto_parts.shape[1], 128))
    sent = [
        jnp.concatenate([proto_parts[o] * jnp.exp2(-power[:, :1]), edge], axis=1).astype(jnp.float16)
        for o in range(1, nb)
    ]
    got = [swap(x, o + 1, 0, 0) for o, x in enumerate(sent)]
    got, mine = lax.optimization_barrier((got, mine))
    ready = [x.astype(jnp.float32) for x in got]
    grad_proto = place(at, [proto_parts[0]] + ready)
    outs = [mine[0]] + [swap(mine[o], o, 0, 0) for o in range(1, nb)]
    grad_student, loss = finish_crops(outs, grain, crops)
    return (grad_proto, grad_student, loss[0, 0])


def solution(mesh):
    in_specs = (P("proto", "batch"), P("proto", "batch"), P("batch", "proto"))
    out_specs = (P("batch", "proto"), P("proto", "batch"), P())
    return jax.shard_map(shards, mesh=mesh, in_specs=in_specs, out_specs=out_specs, check_vma=False)
```

```python
import functools
import math

import jax
import jax.numpy as jnp
from jax import lax
from jax.experimental import pallas as pl
from jax.experimental.pallas import tpu as pltpu
from jax.sharding import PartitionSpec as P


ITERS = 3
CORES = 2
AXES = ("batch", "proto")

teacher_temp = 0.07
student_temp = 0.1
epsilon = 1e-06
LOG2E = 1.0 / math.log(2.0)
T_GAIN = LOG2E / teacher_temp
S_GAIN = LOG2E / student_temp

SMEM = pl.BlockSpec(memory_space=pltpu.SMEM)
VMEM = pl.BlockSpec(memory_space=pltpu.VMEM)


def params(megabytes=24):
    return pltpu.CompilerParams(vmem_limit_bytes=megabytes << 20)


def swap(x, over_batch, over_z, over_core):
    batch, proto = lax.axis_size("batch"), lax.axis_size("proto")
    pairs = []
    for b in range(batch):
        for p in range(proto):
            other = p ^ (over_z * CORES + over_core)
            pairs.append((b * proto + p, (b ^ over_batch) * proto + other))
    return lax.ppermute(x, AXES, pairs)


def z_masks(nz):
    return [1 << i for i in range(nz.bit_length() - 1)]


def join(parts):
    return jnp.concatenate(parts, axis=0)


def gather_crops(teacher, student):
    batch = lax.axis_size("batch")
    nz = lax.axis_size("proto") // CORES
    both = jnp.stack([teacher, student])
    passed = [both] + [swap(both, 0, o, 0) for o in range(1, nz)]
    found = []
    for which in range(2):
        mine = join([x[which][None] for x in passed])[None]
        pieces = join([mine] + [swap(mine, o, 0, 0) for o in range(1, batch)])
        found.append([pieces, swap(pieces, 0, 0, 1)])
    return found


def unit_crops_body(at_ref, *refs):
    pieces, (unit_ref, scale_ref, raw, sems) = refs[:CORES], refs[CORES:]
    j, z, c = at_ref[0], at_ref[1], at_ref[2]
    copies = []
    for core, ref in enumerate(pieces):
        batch, nz, rows, cols = ref.shape
        for ob in range(batch):
            left = pl.multiple_of((j ^ ob) * cols, cols)
            for oz in range(nz):
                top = pl.multiple_of(((z ^ oz) * CORES + (c ^ core)) * rows, rows)
                target = raw.at[pl.ds(top, rows), pl.ds(left, cols)]
                copies.append(pltpu.make_async_copy(ref.at[ob, oz], target, sems.at[len(copies)]))
                copies[-1].start()
    for copy in copies:
        copy.wait()
    for left in range(0, raw.shape[1], cols):
        part = slice(left, left + cols)
        values = raw[:, part].astype(jnp.float32)
        factor = lax.rsqrt(jnp.sum(values * values, axis=0, keepdims=True) + epsilon)
        unit_ref[:, part] = (values * factor).astype(jnp.bfloat16)
        scale_ref[:, part] = factor


def unit_crops(at, found, width, crops, megabytes):
    copies = CORES * found[0].shape[0] * found[0].shape[1]
    return pl.pallas_call(
        unit_crops_body,
        out_shape=(
            jax.ShapeDtypeStruct((width, crops), jnp.bfloat16),
            jax.ShapeDtypeStruct((1, crops), jnp.float32),
        ),
        in_specs=[SMEM] + [pl.BlockSpec(memory_space=pltpu.HBM)] * len(found),
        out_specs=(VMEM, VMEM),
        scratch_shapes=[
            pltpu.VMEM((width, crops), jnp.bfloat16),
            pltpu.SemaphoreType.DMA((copies,)),
        ],
        compiler_params=params(megabytes),
    )(at, *found)


def unit_protos_body(at_ref, *refs):
    blocks, (turned_ref, scale_ref, raw) = refs[:-3], refs[-3:]
    j = at_ref[0]
    rows, step = blocks[0].shape[0], raw.shape[1]
    for low in range(0, blocks[0].shape[1], step):
        part = slice(low, low + step)
        for o, ref in enumerate(blocks):
            top = pl.multiple_of((j ^ o) * rows, rows)
            raw[pl.ds(top, rows), :] = ref[:, part]
        values = raw[...].astype(jnp.float32)
        factor = lax.rsqrt(jnp.sum(values * values, axis=0, keepdims=True) + epsilon)
        turned_ref[part, :] = (values * factor).astype(jnp.bfloat16).T
        scale_ref[:, part] = factor


def unit_protos(at, blocks):
    rows, protos = blocks[0].shape
    width = rows * len(blocks)
    return pl.pallas_call(
        unit_protos_body,
        out_shape=(
            jax.ShapeDtypeStruct((protos, width), jnp.bfloat16),
            jax.ShapeDtypeStruct((1, protos), jnp.float32),
        ),
        in_specs=[SMEM] + [VMEM] * len(blocks),
        out_specs=(VMEM, VMEM),
        scratch_shapes=[pltpu.VMEM((width, min(512, protos)), jnp.bfloat16)],
        compiler_params=params(),
        name="up",
    )(at, *blocks)


def to_row(row_ref, tiles):
    for q in range(tiles.shape[0]):
        row_ref[:, q * 128 : (q + 1) * 128] = tiles[q : q + 1, :]


def to_tiles(tiles_ref, row_ref):
    for q in range(tiles_ref.shape[0]):
        tiles_ref[q : q + 1, :] = row_ref[:, q * 128 : (q + 1) * 128]


def received(got_ref, n):
    cores = []
    for core in range(CORES):
        total = got_ref[core, n]
        for device in range(core + CORES, got_ref.shape[0], CORES):
            total = total + got_ref[device, n]
        cores.append(total)
    return jnp.concatenate(cores, axis=0)


def sweep_body(gain, weigh, before, invert, turned_ref, unit_ref, *refs):
    if weigh:
        got_ref, *refs = refs
        if before:
            before_ref, *refs = refs
        sums_ref, crop_out, *refs = refs
        if invert:
            inv_ref, *refs = refs
        crop_row, total = refs
        crop = 1.0 / received(got_ref, 0)
        if before:
            crop = before_ref[...] * crop
        crop_out[...] = crop
        to_row(crop_row, crop)
    else:
        sums_ref, total = refs
    protos = turned_ref.shape[0]
    step = min(512, protos)
    total[...] = jnp.zeros_like(total)

    def block(i, carry):
        part = pl.ds(pl.multiple_of(i * step, step), step)
        mass = jnp.exp2(jnp.dot(turned_ref[part, :], unit_ref[...], preferred_element_type=jnp.float32) * gain)
        if weigh:
            mass = mass * crop_row[...]
        if gain == T_GAIN:
            inv = 1.0 / jnp.sum(mass, axis=1, keepdims=True)
            if invert:
                inv_ref[:, part] = inv.T
            mass = mass * inv
        total[...] += jnp.sum(mass.reshape(step // 8, 8, mass.shape[1]), axis=0)
        return carry

    lax.fori_loop(0, protos // step, block, 0)
    total[0:1, :] = jnp.sum(total[...], axis=0, keepdims=True)
    to_tiles(sums_ref, total.at[0:1, :])


def sweep(gain, turned, unit, got=None, before=None, invert=False):
    crops = unit.shape[1]
    tiles = jax.ShapeDtypeStruct((crops // 128, 128), jnp.float32)
    weigh = got is not None
    operands = [x for x in (turned, unit, got, before) if x is not None]
    out_shape = [tiles] + [tiles] * weigh
    if invert:
        out_shape.append(jax.ShapeDtypeStruct((1, turned.shape[0]), jnp.float32))
    row = pltpu.VMEM((1, crops), jnp.float32)
    return pl.pallas_call(
        functools.partial(sweep_body, gain, weigh, before is not None, invert),
        out_shape=out_shape,
        in_specs=[VMEM] * len(operands),
        out_specs=[VMEM] * len(out_shape),
        scratch_shapes=[row] * weigh + [pltpu.VMEM((8, crops), jnp.float32)],
        compiler_params=params(),
    )(*operands)


def prepare_body(grain, turned_ref, inv_ref, got_ref, before_ref, protos, inverse, crop_row, total_row):
    to_row(crop_row, jnp.log2(before_ref[...] / (received(got_ref, 0) * grain)))
    to_row(total_row, -jnp.log2(received(got_ref, 1) * grain))
    count = turned_ref.shape[0]
    chunk = min(256, count)
    for low in range(0, count, chunk):
        part = slice(low, low + chunk)
        protos[:, part] = turned_ref[part, :].T
        inverse[part, :] = jnp.broadcast_to(inv_ref[:, part], (128, chunk)).T


def prepare(turned, inv, got, before, grain):
    count, width = turned.shape
    crops = before.shape[0] * 128
    return pl.pallas_call(
        functools.partial(prepare_body, grain),
        out_shape=[
            jax.ShapeDtypeStruct((width, count), jnp.bfloat16),
            jax.ShapeDtypeStruct((count, 128), jnp.float32),
            jax.ShapeDtypeStruct((1, crops), jnp.float32),
            jax.ShapeDtypeStruct((1, crops), jnp.float32),
        ],
        in_specs=[VMEM] * 4,
        out_specs=[VMEM] * 4,
        compiler_params=params(16),
        name="pr",
    )(turned, inv, got, before)


def grads_body(plan, at_ref, turned_ref, protos_ref, inverse_ref, *refs):
    nz, first, blocks, rows, chunk, tile, end = plan
    if first:
        before_ref, loss_before_ref, *refs = refs
    crop_ref, total_ref, teacher_ref, student_ref, crop_scale_ref, crop_out, by_proto, loss_sum, grad_ref, result = refs
    j, z, c = at_ref[0], at_ref[1], at_ref[2]
    count = turned_ref.shape[0]
    cols = crop_out.shape[2]
    loss = loss_before_ref[...] if first else jnp.zeros_like(loss_sum)
    for step in range(blocks * cols // tile):
        block, within = divmod(step * tile, cols)
        here = pl.ds(pl.multiple_of((j ^ (first + block)) * cols + within, tile), tile)
        teacher, student = teacher_ref[:, here], student_ref[:, here]
        crop, total = crop_ref[:, here], total_ref[:, here]
        grads = grad_ref.at[step % 2]
        for low in range(0, count, chunk):
            part = slice(low, low + chunk)
            turned = turned_ref[part, :]
            by_teacher = jnp.dot(turned, teacher, preferred_element_type=jnp.float32)
            by_student = jnp.dot(turned, student, preferred_element_type=jnp.float32)
            inv = jnp.concatenate([inverse_ref[part, :]] * (tile // 128), axis=1)
            targets = jnp.exp2(by_teacher * T_GAIN + crop) * inv
            power = by_student * S_GAIN + total
            grads[part, :] = (jnp.exp2(power) - targets).astype(jnp.bfloat16)
            loss += jnp.sum((targets * power).reshape(chunk // 8, 8, tile), axis=0)
        by_crop = jnp.dot(protos_ref[...], grads[...], preferred_element_type=jnp.float32)
        values = student.astype(jnp.float32)
        radial = jnp.sum(values * by_crop, axis=0, keepdims=True)
        result[step % 2] = (by_crop - values * radial) * crop_scale_ref[:, here]
        for oc in range(CORES):
            for oz in range(nz):
                top = pl.multiple_of(((z ^ oz) * CORES + (c ^ oc)) * rows, rows)
                low = (oz * blocks + block) * rows
                crop_out[oc, low : low + rows, within : within + tile] = result[step % 2, pl.ds(top, rows), :]
        turned_student = student.T
        for low in range(0, count, chunk):
            part = slice(low, low + chunk)
            more = jnp.dot(grads[part, :], turned_student, preferred_element_type=jnp.float32)
            old = by_proto if step else before_ref if first else None
            by_proto[part, :] = more if old is None else old[part, :] + more
    loss_sum[...] = loss
    if end:
        total = jnp.sum(jnp.sum(loss, axis=0, keepdims=True), axis=1, keepdims=True)
        for oc in range(CORES):
            crop_out[oc, -8:, :] = jnp.broadcast_to(total, (8, cols))


def gradients(at, sizes, group, groups, turned, prepared, sums, teacher, student, crop_scale):
    nb, nz = sizes
    count, width = turned.shape
    crops = teacher.shape[1]
    rows, cols = width // (nz * CORES), crops // nb
    blocks = nb // groups
    tile = min(256, cols)
    chunk = min(256, count)
    end = group == groups - 1
    protos, inverse, crop_row, total_row = prepared
    operands = [turned, protos, inverse] + list(sums) + [crop_row, total_row, teacher, student, crop_scale]
    return pl.pallas_call(
        functools.partial(grads_body, (nz, group * blocks, blocks, rows, chunk, tile, end)),
        in_specs=[SMEM] + [VMEM] * len(operands),
        out_specs=[VMEM, VMEM, VMEM],
        scratch_shapes=[
            pltpu.VMEM((2, count, tile), jnp.bfloat16),
            pltpu.VMEM((2, width, tile), jnp.float32),
        ],
        out_shape=[
            jax.ShapeDtypeStruct((CORES, nz * blocks * rows + 8 * end, cols), jnp.float32),
            jax.ShapeDtypeStruct((count, width), jnp.float32),
            jax.ShapeDtypeStruct((8, tile), jnp.float32),
        ],
        compiler_params=params(20),
    )(at, *operands)


def finish_protos_body(nb, at_ref, by_proto, turned_ref, scale_ref, out_ref, top_ref, result):
    j = at_ref[0]
    count, width = by_proto.shape
    chunk = result.shape[1]
    wide = width // nb
    tops = jnp.zeros((1, chunk), jnp.float32)
    for low in range(0, count, chunk):
        part = slice(low, low + chunk)
        total = by_proto[part, :]
        values = turned_ref[part, :].astype(jnp.float32)
        radial = jnp.sum(values * total, axis=1, keepdims=True)
        final = (total - values * radial).T * scale_ref[:, part]
        result[...] = final
        tops = jnp.maximum(tops, jnp.max(jnp.abs(final), axis=0, keepdims=True))
        for o in range(nb):
            out_ref[o, :, part] = result[pl.ds(pl.multiple_of((j ^ o) * wide, wide), wide), :]
    top_ref[...] = jnp.broadcast_to(jnp.max(tops, axis=1, keepdims=True), top_ref.shape)


def finish_protos(at, nb, by_proto, turned, scale):
    count, width = turned.shape
    return pl.pallas_call(
        functools.partial(finish_protos_body, nb),
        out_shape=[
            jax.ShapeDtypeStruct((nb, width // nb, count), jnp.float32),
            jax.ShapeDtypeStruct((1, 128), jnp.float32),
        ],
        in_specs=[SMEM, VMEM, VMEM, VMEM],
        out_specs=[VMEM, VMEM],
        scratch_shapes=[pltpu.VMEM((width, min(256, count)), jnp.float32)],
        compiler_params=params(),
        name="fp",
    )(at, by_proto, turned, scale)


def finish_crops_body(grain, crops, *refs):
    parts, (grad_ref, loss_ref) = refs[:-2], refs[-2:]
    total = parts[0][...]
    for ref in parts[1:]:
        total = total + ref[...]
    rows = grad_ref.shape[0]
    grad_ref[...] = total[:rows]
    loss_ref[...] = (total[rows : rows + 1, :128] * grain + math.log2(grain) * crops) * (-1.0 / (LOG2E * crops))


def finish_crops(parts, grain, crops):
    rows, cols = parts[0].shape
    return pl.pallas_call(
        functools.partial(finish_crops_body, grain, crops),
        out_shape=[
            jax.ShapeDtypeStruct((rows - 8, cols), jnp.float32),
            jax.ShapeDtypeStruct((1, 128), jnp.float32),
        ],
        in_specs=[VMEM] * len(parts),
        out_specs=[VMEM, VMEM],
        compiler_params=params(4),
        name="fc",
    )(*parts)


def pack_body(at_ref, *refs):
    mine, theirs, out_ref = refs[: len(refs) // 2], refs[len(refs) // 2 : -1], refs[-1]
    half = out_ref.shape[2]
    part = pl.ds(pl.multiple_of(at_ref[2] * half, half), half)
    for n in range(len(mine)):
        total = mine[n][part, :] + theirs[n][part, :]
        for device in range(out_ref.shape[0]):
            out_ref[device, n] = total


def sum_everywhere(at, *tiles):
    devices = lax.axis_size("batch") * lax.axis_size("proto")
    theirs = [swap(x, 0, 0, 1) for x in tiles]
    sent = pl.pallas_call(
        pack_body,
        out_shape=jax.ShapeDtypeStruct((devices, len(tiles), tiles[0].shape[0] // CORES, 128), jnp.float32),
        in_specs=[SMEM] + [VMEM] * (2 * len(tiles)),
        out_specs=VMEM,
        compiler_params=params(),
        name="pk",
    )(at, *tiles, *theirs)
    return lax.all_to_all(sent, AXES, 0, 0)


def scatter_crops(parts, nz, rows):
    kept = parts[0] + swap(parts[1], 0, 0, 1)
    blocks = kept.shape[0] // (nz * rows)
    size = blocks * rows
    extra = kept[nz * size :]
    held = {o: kept[o * size : (o + 1) * size] for o in range(nz)}
    masks = z_masks(nz)
    for i, mask in enumerate(masks):
        span = [0]
        for later in masks[i + 1 :]:
            span = span + [o ^ later for o in span]
        sent = [held[o ^ mask] for o in span] + [extra] * bool(extra.shape[0])
        got = swap(jnp.concatenate(sent, axis=0), 0, mask, 0)
        held = {o: held[o] + got[n * size : (n + 1) * size] for n, o in enumerate(span)}
        extra = extra + got[len(span) * size :]
        held, extra = lax.optimization_barrier((held, extra))
    return [held[0][i * rows : (i + 1) * rows] for i in range(blocks)], extra


def place_body(at_ref, *refs):
    parts, (out_ref, scaled, sems) = refs[:-3], refs[-3:]
    cols = parts[0].shape[1]
    copies = []
    for o, ref in enumerate(parts):
        left = pl.multiple_of((at_ref[0] ^ o) * cols, cols)
        source = ref
        if o:
            source = scaled.at[o - 1]
            gain = jnp.exp2(ref[:, cols:])
            source[...] = ref[:, :cols] * jnp.concatenate([gain] * (cols // 128), axis=1)
        copies.append(pltpu.make_async_copy(source, out_ref.at[:, pl.ds(left, cols)], sems.at[o]))
        copies[-1].start()
    for copy in copies:
        copy.wait()


def place(at, parts):
    rows, cols = parts[0].shape
    return pl.pallas_call(
        place_body,
        out_shape=jax.ShapeDtypeStruct((rows, cols * len(parts)), jnp.float32),
        in_specs=[SMEM] + [VMEM] * len(parts),
        out_specs=pl.BlockSpec(memory_space=pl.ANY),
        scratch_shapes=[
            pltpu.VMEM((len(parts) - 1, rows, cols), jnp.float32),
            pltpu.SemaphoreType.DMA((len(parts),)),
        ],
        compiler_params=params(16),
        name="pl",
    )(at, *parts)


def shards(teacher_emb, student_emb, prototypes):
    nb, nproto = lax.axis_size("batch"), lax.axis_size("proto")
    nz = nproto // CORES
    j, p = lax.axis_index("batch"), lax.axis_index("proto")
    at = jnp.stack([j, p // CORES, p % CORES]).astype(jnp.int32)
    width = teacher_emb.shape[0] * nproto
    crops = teacher_emb.shape[1] * nb
    count = prototypes.shape[1] // nb
    grain = crops * student_temp

    prototypes, at = lax.optimization_barrier((prototypes, at))

    def columns(o):
        return lax.dynamic_slice_in_dim(prototypes, (j ^ o) * count, count, 1)

    blocks = [columns(0)] + [swap(columns(o), o, 0, 0) for o in range(1, nb)]
    turned, proto_scale = unit_protos(at, blocks)
    found = gather_crops(teacher_emb, student_emb)
    teacher = unit_crops(at, found[0], width, crops, 24)[0]
    student, crop_unit_scale = unit_crops(at, found[1], width, crops, 60)

    (sums,) = sweep(T_GAIN, turned, teacher)
    got, crop, inv = sum_everywhere(at, sums), None, []
    for iteration in range(1, ITERS):
        final = iteration == ITERS - 1
        sums, crop, *inv = sweep(T_GAIN, turned, teacher, got, crop, invert=final)
        if final:
            got = sum_everywhere(at, sums, softmax_total)
        else:
            got = sum_everywhere(at, sums)
            (softmax_total,) = sweep(S_GAIN, turned, student)
    prepared = prepare(turned, inv[0], got, crop, grain)
    groups = min(4, nb)
    mine, sums = [], []
    for group in range(groups):
        crop_parts, *sums = gradients(
            at, (nb, nz), group, groups, turned, prepared, sums, teacher, student, crop_unit_scale
        )
        more, extra = scatter_crops(crop_parts, nz, teacher_emb.shape[0])
        mine += more
    by_proto = sums[0]
    mine = [jnp.concatenate([part, extra], axis=0) for part in mine]
    proto_parts, top = finish_protos(at, nb, by_proto, turned, proto_scale)
    power = jnp.ceil(jnp.log2(jnp.maximum(top, 1e-30))) - 15.0
    edge = jnp.broadcast_to(power, (proto_parts.shape[1], 128))
    sent = [
        jnp.concatenate([proto_parts[o] * jnp.exp2(-power[:, :1]), edge], axis=1).astype(jnp.float16)
        for o in range(1, nb)
    ]
    got = [swap(x, o + 1, 0, 0) for o, x in enumerate(sent)]
    got, mine = lax.optimization_barrier((got, mine))
    ready = [x.astype(jnp.float32) for x in got]
    grad_proto = place(at, [proto_parts[0]] + ready)
    outs = [mine[0]] + [swap(mine[o], o, 0, 0) for o in range(1, nb)]
    grad_student, loss = finish_crops(outs, grain, crops)
    return (grad_proto, grad_student, loss[0, 0])


def solution(mesh):
    in_specs = (P("proto", "batch"), P("proto", "batch"), P("batch", "proto"))
    out_specs = (P("batch", "proto"), P("proto", "batch"), P())
    return jax.shard_map(shards, mesh=mesh, in_specs=in_specs, out_specs=out_specs, check_vma=False)
```

```python
import functools
import math

import jax
import jax.numpy as jnp
from jax import lax
from jax.experimental import pallas as pl
from jax.experimental.pallas import tpu as pltpu
from jax.sharding import PartitionSpec as P


ITERS = 3
CORES = 2
AXES = ("batch", "proto")

teacher_temp = 0.07
student_temp = 0.1
epsilon = 1e-06
LOG2E = 1.0 / math.log(2.0)
T_GAIN = LOG2E / teacher_temp
S_GAIN = LOG2E / student_temp

SMEM = pl.BlockSpec(memory_space=pltpu.SMEM)
VMEM = pl.BlockSpec(memory_space=pltpu.VMEM)


def params(megabytes=24):
    return pltpu.CompilerParams(vmem_limit_bytes=megabytes << 20)


def swap(x, over_batch, over_z, over_core):
    batch, proto = lax.axis_size("batch"), lax.axis_size("proto")
    pairs = []
    for b in range(batch):
        for p in range(proto):
            other = p ^ (over_z * CORES + over_core)
            pairs.append((b * proto + p, (b ^ over_batch) * proto + other))
    return lax.ppermute(x, AXES, pairs)


def z_masks(nz):
    return [1 << i for i in range(nz.bit_length() - 1)]


def join(parts):
    return jnp.concatenate(parts, axis=0)


def gather_crops(teacher, student):
    batch = lax.axis_size("batch")
    nz = lax.axis_size("proto") // CORES
    both = jnp.stack([teacher, student])
    passed = [both] + [swap(both, 0, o, 0) for o in range(1, nz)]
    found = []
    for which in range(2):
        mine = join([x[which][None] for x in passed])[None]
        pieces = join([mine] + [swap(mine, o, 0, 0) for o in range(1, batch)])
        found.append([pieces, swap(pieces, 0, 0, 1)])
    return found


def unit_crops_body(at_ref, *refs):
    pieces, (unit_ref, scale_ref, raw, sems) = refs[:CORES], refs[CORES:]
    j, z, c = at_ref[0], at_ref[1], at_ref[2]
    copies = []
    for core, ref in enumerate(pieces):
        batch, nz, rows, cols = ref.shape
        for ob in range(batch):
            left = pl.multiple_of((j ^ ob) * cols, cols)
            for oz in range(nz):
                top = pl.multiple_of(((z ^ oz) * CORES + (c ^ core)) * rows, rows)
                target = raw.at[pl.ds(top, rows), pl.ds(left, cols)]
                copies.append(pltpu.make_async_copy(ref.at[ob, oz], target, sems.at[len(copies)]))
                copies[-1].start()
    for copy in copies:
        copy.wait()
    for left in range(0, raw.shape[1], cols):
        part = slice(left, left + cols)
        values = raw[:, part].astype(jnp.float32)
        factor = lax.rsqrt(jnp.sum(values * values, axis=0, keepdims=True) + epsilon)
        unit_ref[:, part] = (values * factor).astype(jnp.bfloat16)
        scale_ref[:, part] = factor


def unit_crops(at, found, width, crops, megabytes):
    copies = CORES * found[0].shape[0] * found[0].shape[1]
    return pl.pallas_call(
        unit_crops_body,
        out_shape=(
            jax.ShapeDtypeStruct((width, crops), jnp.bfloat16),
            jax.ShapeDtypeStruct((1, crops), jnp.float32),
        ),
        in_specs=[SMEM] + [pl.BlockSpec(memory_space=pltpu.HBM)] * len(found),
        out_specs=(VMEM, VMEM),
        scratch_shapes=[
            pltpu.VMEM((width, crops), jnp.bfloat16),
            pltpu.SemaphoreType.DMA((copies,)),
        ],
        compiler_params=params(megabytes),
    )(at, *found)


def unit_protos_body(at_ref, *refs):
    blocks, (turned_ref, scale_ref, raw) = refs[:-3], refs[-3:]
    j = at_ref[0]
    rows, step = blocks[0].shape[0], raw.shape[1]
    for low in range(0, blocks[0].shape[1], step):
        part = slice(low, low + step)
        for o, ref in enumerate(blocks):
            top = pl.multiple_of((j ^ o) * rows, rows)
            raw[pl.ds(top, rows), :] = ref[:, part]
        values = raw[...].astype(jnp.float32)
        factor = lax.rsqrt(jnp.sum(values * values, axis=0, keepdims=True) + epsilon)
        turned_ref[part, :] = (values * factor).astype(jnp.bfloat16).T
        scale_ref[:, part] = factor


def unit_protos(at, blocks):
    rows, protos = blocks[0].shape
    width = rows * len(blocks)
    return pl.pallas_call(
        unit_protos_body,
        out_shape=(
            jax.ShapeDtypeStruct((protos, width), jnp.bfloat16),
            jax.ShapeDtypeStruct((1, protos), jnp.float32),
        ),
        in_specs=[SMEM] + [VMEM] * len(blocks),
        out_specs=(VMEM, VMEM),
        scratch_shapes=[pltpu.VMEM((width, min(512, protos)), jnp.bfloat16)],
        compiler_params=params(),
        name="up",
    )(at, *blocks)


def to_row(row_ref, tiles):
    for q in range(tiles.shape[0]):
        row_ref[:, q * 128 : (q + 1) * 128] = tiles[q : q + 1, :]


def to_tiles(tiles_ref, row_ref):
    for q in range(tiles_ref.shape[0]):
        tiles_ref[q : q + 1, :] = row_ref[:, q * 128 : (q + 1) * 128]


def received(got_ref, n):
    cores = []
    for core in range(CORES):
        total = got_ref[core, n]
        for device in range(core + CORES, got_ref.shape[0], CORES):
            total = total + got_ref[device, n]
        cores.append(total)
    return jnp.concatenate(cores, axis=0)


def sweep_body(gain, weigh, before, invert, turned_ref, unit_ref, *refs):
    if weigh:
        got_ref, *refs = refs
        if before:
            before_ref, *refs = refs
        sums_ref, crop_out, *refs = refs
        if invert:
            inv_ref, *refs = refs
        crop_row, total = refs
        crop = 1.0 / received(got_ref, 0)
        if before:
            crop = before_ref[...] * crop
        crop_out[...] = crop
        to_row(crop_row, crop)
    else:
        sums_ref, total = refs
    protos = turned_ref.shape[0]
    step = min(1024, protos)
    total[...] = jnp.zeros_like(total)

    def block(i, carry):
        part = pl.ds(pl.multiple_of(i * step, step), step)
        mass = jnp.exp2(jnp.dot(turned_ref[part, :], unit_ref[...], preferred_element_type=jnp.float32) * gain)
        if weigh:
            mass = mass * crop_row[...]
        if gain == T_GAIN:
            inv = 1.0 / jnp.sum(mass, axis=1, keepdims=True)
            if invert:
                inv_ref[:, part] = inv.T
            mass = mass * inv
        total[...] += jnp.sum(mass.reshape(step // 8, 8, mass.shape[1]), axis=0)
        return carry

    lax.fori_loop(0, protos // step, block, 0)
    total[0:1, :] = jnp.sum(total[...], axis=0, keepdims=True)
    to_tiles(sums_ref, total.at[0:1, :])


def sweep(gain, turned, unit, got=None, before=None, invert=False):
    crops = unit.shape[1]
    tiles = jax.ShapeDtypeStruct((crops // 128, 128), jnp.float32)
    weigh = got is not None
    operands = [x for x in (turned, unit, got, before) if x is not None]
    out_shape = [tiles] + [tiles] * weigh
    if invert:
        out_shape.append(jax.ShapeDtypeStruct((1, turned.shape[0]), jnp.float32))
    row = pltpu.VMEM((1, crops), jnp.float32)
    return pl.pallas_call(
        functools.partial(sweep_body, gain, weigh, before is not None, invert),
        out_shape=out_shape,
        in_specs=[VMEM] * len(operands),
        out_specs=[VMEM] * len(out_shape),
        scratch_shapes=[row] * weigh + [pltpu.VMEM((8, crops), jnp.float32)],
        compiler_params=params(),
    )(*operands)


def prepare_body(grain, turned_ref, inv_ref, got_ref, before_ref, protos, inverse, crop_row, total_row):
    to_row(crop_row, jnp.log2(before_ref[...] / (received(got_ref, 0) * grain)))
    to_row(total_row, -jnp.log2(received(got_ref, 1) * grain))
    count = turned_ref.shape[0]
    chunk = min(256, count)
    for low in range(0, count, chunk):
        part = slice(low, low + chunk)
        protos[:, part] = turned_ref[part, :].T
        inverse[part, :] = jnp.broadcast_to(inv_ref[:, part], (128, chunk)).T


def prepare(turned, inv, got, before, grain):
    count, width = turned.shape
    crops = before.shape[0] * 128
    return pl.pallas_call(
        functools.partial(prepare_body, grain),
        out_shape=[
            jax.ShapeDtypeStruct((width, count), jnp.bfloat16),
            jax.ShapeDtypeStruct((count, 128), jnp.float32),
            jax.ShapeDtypeStruct((1, crops), jnp.float32),
            jax.ShapeDtypeStruct((1, crops), jnp.float32),
        ],
        in_specs=[VMEM] * 4,
        out_specs=[VMEM] * 4,
        compiler_params=params(16),
        name="pr",
    )(turned, inv, got, before)


def grads_body(plan, at_ref, turned_ref, protos_ref, inverse_ref, *refs):
    nz, first, blocks, rows, chunk, tile, end = plan
    if first:
        before_ref, loss_before_ref, *refs = refs
    crop_ref, total_ref, teacher_ref, student_ref, crop_scale_ref, crop_out, by_proto, loss_sum, grad_ref, result = refs
    j, z, c = at_ref[0], at_ref[1], at_ref[2]
    count = turned_ref.shape[0]
    cols = crop_out.shape[2]
    loss = loss_before_ref[...] if first else jnp.zeros_like(loss_sum)
    for step in range(blocks * cols // tile):
        block, within = divmod(step * tile, cols)
        here = pl.ds(pl.multiple_of((j ^ (first + block)) * cols + within, tile), tile)
        teacher, student = teacher_ref[:, here], student_ref[:, here]
        crop, total = crop_ref[:, here], total_ref[:, here]
        grads = grad_ref.at[step % 2]
        for low in range(0, count, chunk):
            part = slice(low, low + chunk)
            turned = turned_ref[part, :]
            by_teacher = jnp.dot(turned, teacher, preferred_element_type=jnp.float32)
            by_student = jnp.dot(turned, student, preferred_element_type=jnp.float32)
            inv = jnp.concatenate([inverse_ref[part, :]] * (tile // 128), axis=1)
            targets = jnp.exp2(by_teacher * T_GAIN + crop) * inv
            power = by_student * S_GAIN + total
            grads[part, :] = (jnp.exp2(power) - targets).astype(jnp.bfloat16)
            loss += jnp.sum((targets * power).reshape(chunk // 8, 8, tile), axis=0)
        by_crop = jnp.dot(protos_ref[...], grads[...], preferred_element_type=jnp.float32)
        values = student.astype(jnp.float32)
        radial = jnp.sum(values * by_crop, axis=0, keepdims=True)
        result[step % 2] = (by_crop - values * radial) * crop_scale_ref[:, here]
        for oc in range(CORES):
            for oz in range(nz):
                top = pl.multiple_of(((z ^ oz) * CORES + (c ^ oc)) * rows, rows)
                low = (oz * blocks + block) * rows
                crop_out[oc, low : low + rows, within : within + tile] = result[step % 2, pl.ds(top, rows), :]
        turned_student = student.T
        for low in range(0, count, chunk):
            part = slice(low, low + chunk)
            more = jnp.dot(grads[part, :], turned_student, preferred_element_type=jnp.float32)
            old = by_proto if step else before_ref if first else None
            by_proto[part, :] = more if old is None else old[part, :] + more
    loss_sum[...] = loss
    if end:
        total = jnp.sum(jnp.sum(loss, axis=0, keepdims=True), axis=1, keepdims=True)
        for oc in range(CORES):
            crop_out[oc, -8:, :] = jnp.broadcast_to(total, (8, cols))


def gradients(at, sizes, group, groups, turned, prepared, sums, teacher, student, crop_scale):
    nb, nz = sizes
    count, width = turned.shape
    crops = teacher.shape[1]
    rows, cols = width // (nz * CORES), crops // nb
    blocks = nb // groups
    tile = min(256, cols)
    chunk = min(256, count)
    end = group == groups - 1
    protos, inverse, crop_row, total_row = prepared
    operands = [turned, protos, inverse] + list(sums) + [crop_row, total_row, teacher, student, crop_scale]
    return pl.pallas_call(
        functools.partial(grads_body, (nz, group * blocks, blocks, rows, chunk, tile, end)),
        in_specs=[SMEM] + [VMEM] * len(operands),
        out_specs=[VMEM, VMEM, VMEM],
        scratch_shapes=[
            pltpu.VMEM((2, count, tile), jnp.bfloat16),
            pltpu.VMEM((2, width, tile), jnp.float32),
        ],
        out_shape=[
            jax.ShapeDtypeStruct((CORES, nz * blocks * rows + 8 * end, cols), jnp.float32),
            jax.ShapeDtypeStruct((count, width), jnp.float32),
            jax.ShapeDtypeStruct((8, tile), jnp.float32),
        ],
        compiler_params=params(20),
    )(at, *operands)


def finish_protos_body(nb, at_ref, by_proto, turned_ref, scale_ref, out_ref, top_ref, result):
    j = at_ref[0]
    count, width = by_proto.shape
    chunk = result.shape[1]
    wide = width // nb
    tops = jnp.zeros((1, chunk), jnp.float32)
    for low in range(0, count, chunk):
        part = slice(low, low + chunk)
        total = by_proto[part, :]
        values = turned_ref[part, :].astype(jnp.float32)
        radial = jnp.sum(values * total, axis=1, keepdims=True)
        final = (total - values * radial).T * scale_ref[:, part]
        result[...] = final
        tops = jnp.maximum(tops, jnp.max(jnp.abs(final), axis=0, keepdims=True))
        for o in range(nb):
            out_ref[o, :, part] = result[pl.ds(pl.multiple_of((j ^ o) * wide, wide), wide), :]
    top_ref[...] = jnp.broadcast_to(jnp.max(tops, axis=1, keepdims=True), top_ref.shape)


def finish_protos(at, nb, by_proto, turned, scale):
    count, width = turned.shape
    return pl.pallas_call(
        functools.partial(finish_protos_body, nb),
        out_shape=[
            jax.ShapeDtypeStruct((nb, width // nb, count), jnp.float32),
            jax.ShapeDtypeStruct((1, 128), jnp.float32),
        ],
        in_specs=[SMEM, VMEM, VMEM, VMEM],
        out_specs=[VMEM, VMEM],
        scratch_shapes=[pltpu.VMEM((width, min(256, count)), jnp.float32)],
        compiler_params=params(),
        name="fp",
    )(at, by_proto, turned, scale)


def finish_crops_body(grain, crops, *refs):
    parts, (grad_ref, loss_ref) = refs[:-2], refs[-2:]
    total = parts[0][...]
    for ref in parts[1:]:
        total = total + ref[...]
    rows = grad_ref.shape[0]
    grad_ref[...] = total[:rows]
    loss_ref[...] = (total[rows : rows + 1, :128] * grain + math.log2(grain) * crops) * (-1.0 / (LOG2E * crops))


def finish_crops(parts, grain, crops):
    rows, cols = parts[0].shape
    return pl.pallas_call(
        functools.partial(finish_crops_body, grain, crops),
        out_shape=[
            jax.ShapeDtypeStruct((rows - 8, cols), jnp.float32),
            jax.ShapeDtypeStruct((1, 128), jnp.float32),
        ],
        in_specs=[VMEM] * len(parts),
        out_specs=[VMEM, VMEM],
        compiler_params=params(4),
        name="fc",
    )(*parts)


def pack_body(at_ref, *refs):
    mine, theirs, out_ref = refs[: len(refs) // 2], refs[len(refs) // 2 : -1], refs[-1]
    half = out_ref.shape[2]
    part = pl.ds(pl.multiple_of(at_ref[2] * half, half), half)
    for n in range(len(mine)):
        total = mine[n][part, :] + theirs[n][part, :]
        for device in range(out_ref.shape[0]):
            out_ref[device, n] = total


def sum_everywhere(at, *tiles):
    devices = lax.axis_size("batch") * lax.axis_size("proto")
    theirs = [swap(x, 0, 0, 1) for x in tiles]
    sent = pl.pallas_call(
        pack_body,
        out_shape=jax.ShapeDtypeStruct((devices, len(tiles), tiles[0].shape[0] // CORES, 128), jnp.float32),
        in_specs=[SMEM] + [VMEM] * (2 * len(tiles)),
        out_specs=VMEM,
        compiler_params=params(),
        name="pk",
    )(at, *tiles, *theirs)
    return lax.all_to_all(sent, AXES, 0, 0)


def scatter_crops(parts, nz, rows):
    kept = parts[0] + swap(parts[1], 0, 0, 1)
    blocks = kept.shape[0] // (nz * rows)
    size = blocks * rows
    extra = kept[nz * size :]
    held = {o: kept[o * size : (o + 1) * size] for o in range(nz)}
    masks = z_masks(nz)
    for i, mask in enumerate(masks):
        span = [0]
        for later in masks[i + 1 :]:
            span = span + [o ^ later for o in span]
        sent = [held[o ^ mask] for o in span] + [extra] * bool(extra.shape[0])
        got = swap(jnp.concatenate(sent, axis=0), 0, mask, 0)
        held = {o: held[o] + got[n * size : (n + 1) * size] for n, o in enumerate(span)}
        extra = extra + got[len(span) * size :]
        held, extra = lax.optimization_barrier((held, extra))
    return [held[0][i * rows : (i + 1) * rows] for i in range(blocks)], extra


def place_body(at_ref, *refs):
    parts, (out_ref, scaled, sems) = refs[:-3], refs[-3:]
    cols = parts[0].shape[1]
    copies = []
    for o, ref in enumerate(parts):
        left = pl.multiple_of((at_ref[0] ^ o) * cols, cols)
        source = ref
        if o:
            source = scaled.at[o - 1]
            gain = jnp.exp2(ref[:, cols:])
            source[...] = ref[:, :cols] * jnp.concatenate([gain] * (cols // 128), axis=1)
        copies.append(pltpu.make_async_copy(source, out_ref.at[:, pl.ds(left, cols)], sems.at[o]))
        copies[-1].start()
    for copy in copies:
        copy.wait()


def place(at, parts):
    rows, cols = parts[0].shape
    return pl.pallas_call(
        place_body,
        out_shape=jax.ShapeDtypeStruct((rows, cols * len(parts)), jnp.float32),
        in_specs=[SMEM] + [VMEM] * len(parts),
        out_specs=pl.BlockSpec(memory_space=pl.ANY),
        scratch_shapes=[
            pltpu.VMEM((len(parts) - 1, rows, cols), jnp.float32),
            pltpu.SemaphoreType.DMA((len(parts),)),
        ],
        compiler_params=params(16),
        name="pl",
    )(at, *parts)


def shards(teacher_emb, student_emb, prototypes):
    nb, nproto = lax.axis_size("batch"), lax.axis_size("proto")
    nz = nproto // CORES
    j, p = lax.axis_index("batch"), lax.axis_index("proto")
    at = jnp.stack([j, p // CORES, p % CORES]).astype(jnp.int32)
    width = teacher_emb.shape[0] * nproto
    crops = teacher_emb.shape[1] * nb
    count = prototypes.shape[1] // nb
    grain = crops * student_temp

    prototypes, at = lax.optimization_barrier((prototypes, at))

    def columns(o):
        return lax.dynamic_slice_in_dim(prototypes, (j ^ o) * count, count, 1)

    blocks = [columns(0)] + [swap(columns(o), o, 0, 0) for o in range(1, nb)]
    turned, proto_scale = unit_protos(at, blocks)
    found = gather_crops(teacher_emb, student_emb)
    teacher = unit_crops(at, found[0], width, crops, 24)[0]
    student, crop_unit_scale = unit_crops(at, found[1], width, crops, 24)

    (sums,) = sweep(T_GAIN, turned, teacher)
    got, crop, inv = sum_everywhere(at, sums), None, []
    for iteration in range(1, ITERS):
        final = iteration == ITERS - 1
        sums, crop, *inv = sweep(T_GAIN, turned, teacher, got, crop, invert=final)
        if final:
            got = sum_everywhere(at, sums, softmax_total)
        else:
            got = sum_everywhere(at, sums)
            (softmax_total,) = sweep(S_GAIN, turned, student)
    prepared = prepare(turned, inv[0], got, crop, grain)
    groups = min(4, nb)
    mine, sums = [], []
    for group in range(groups):
        crop_parts, *sums = gradients(
            at, (nb, nz), group, groups, turned, prepared, sums, teacher, student, crop_unit_scale
        )
        more, extra = scatter_crops(crop_parts, nz, teacher_emb.shape[0])
        mine += more
    by_proto = sums[0]
    mine = [jnp.concatenate([part, extra], axis=0) for part in mine]
    proto_parts, top = finish_protos(at, nb, by_proto, turned, proto_scale)
    power = jnp.ceil(jnp.log2(jnp.maximum(top, 1e-30))) - 15.0
    edge = jnp.broadcast_to(power, (proto_parts.shape[1], 128))
    sent = [
        jnp.concatenate([proto_parts[o] * jnp.exp2(-power[:, :1]), edge], axis=1).astype(jnp.float16)
        for o in range(1, nb)
    ]
    got = [swap(x, o + 1, 0, 0) for o, x in enumerate(sent)]
    got = lax.optimization_barrier((got, mine))[0]
    ready = [x.astype(jnp.float32) for x in got]
    grad_proto = place(at, [proto_parts[0]] + ready)
    outs = [mine[0]] + [swap(mine[o], o, 0, 0) for o in range(1, nb)]
    grad_student, loss = finish_crops(outs, grain, crops)
    return (grad_proto, grad_student, loss[0, 0])


def solution(mesh):
    in_specs = (P("proto", "batch"), P("proto", "batch"), P("batch", "proto"))
    out_specs = (P("batch", "proto"), P("proto", "batch"), P())
    return jax.shard_map(shards, mesh=mesh, in_specs=in_specs, out_specs=out_specs, check_vma=False)
```
